128 devices in a mesh: wide: 16 (over z, y), narrow: 8 (over x, core).
Axes of the slice: x: 4, y: 4, z: 4, core: 2. Of those that a mesh axis runs over, the one named last changes fastest.
Arguments:
- hidden_in: bfloat16 [2048, 2048], P('wide'), may hold values from -6 to 6
- attn_gain: float32 [2048], replicated, may hold values from 0.1 to 1.9
- w_qkv: bfloat16 [2048, 4096], P('wide', 'narrow'), may hold values from -0.125 to 0.125
- q_gain: float32 [128], replicated, may hold values from 0.5 to 10
- k_gain: float32 [128], replicated, may hold values from 0.1 to 1.9
- w_out: bfloat16 [2048, 2048], P('narrow', 'wide'), may hold values from -0.125 to 0.125
- prefix_cache: bfloat16 [2, 64, 4096, 1024], P(None, 'wide', None, 'narrow'), may hold values from -150 to 150
- tail_cache: bfloat16 [2, 1024, 256, 1024], P(None, 'wide', None, 'narrow'), may hold values from -150 to 150
- prompt_lens: int32 [64], replicated, may hold values from 1 to 4096
- tail_lens: int32 [1024], P('wide'), may hold values from 1 to 256
- slot_prompt: int32 [64], replicated, may hold values from 0 to 63, each once
Outputs:
- hidden_out: bfloat16 [2048, 2048], P('wide')
- scores: float32 [2048, 16], P('wide', 'narrow')
- new_cache: bfloat16 [2, 2048, 1024], P(None, 'wide', 'narrow')
The draws below stay inside these ranges and needn't reach their ends.
Inputs may be any that keep to these rules, and one draw needn't show every extreme that they name: `slot_prompt`: each prompt is held in exactly one slot.
All inputs are finite; a program needn't handle non-finite values.
Results may differ from the reference program's by a relative error of at most 0.007.
Values may be sent and summed in bfloat16 or wider, within the bound.
No kernel may reach another device: no remote copies, remote signals or barrier semaphores. Data moves between devices by JAX's collectives and lax.ppermute only.
A program may use at most 128 MiB of HBM per device.

```python
import math
import jax
import jax.numpy as jnp
from jax import lax

D = 2048
HEADS = 16
KVH = 8
HD = 128
CONT = 16
NEW = 2
PLEN = 4096
TLEN = 256
PROMPTS = 64
CONTS = 1024
ROWS = 2048


def draw_prompt_lens(key, part):
    base_key = jax.random.fold_in(key, 101)
    key_shift, key_extra, key_spot = jax.random.split(base_key, 3)
    shift_by = jax.random.randint(key_shift, (PROMPTS,), 0, 6)
    base_len = jnp.right_shift(jnp.full((PROMPTS,), PLEN, jnp.int32), shift_by)
    extra_len = jax.random.randint(key_extra, (PROMPTS,), 0, 1 << 20) % (base_len // 2 + 1)
    lengths = base_len - base_len // 2 + extra_len
    chosen_spot = jax.random.randint(key_spot, (), 0, PROMPTS)
    return lengths.at[chosen_spot].set(PLEN).astype(jnp.int32)


def draw_tail_lens(key, part):
    base_key = jax.random.fold_in(key, 202)
    key_len, key_spot = jax.random.split(base_key, 2)
    lengths = jax.random.randint(key_len, (CONTS,), 1, TLEN + 1)
    chosen_spot = jax.random.randint(key_spot, (), 0, CONTS)
    return lengths.at[chosen_spot].set(TLEN).astype(jnp.int32)


def cache_entries(base_key, count_rows, length_rows):
    key_keys, key_values = jax.random.split(base_key, 2)
    shape_full = (count_rows, length_rows, KVH, HD)
    keys_part = jnp.clip(jax.random.normal(key_keys, shape_full, jnp.float32), -6.0, 6.0)
    values_part = jnp.clip(jax.random.normal(key_values, shape_full, jnp.float32), -6.0, 6.0)
    stacked = jnp.stack([keys_part.reshape(count_rows, length_rows, KVH * HD), values_part.reshape(count_rows, length_rows, KVH * HD)])
    return stacked.astype(jnp.bfloat16)


def draw_prefix_cache(key, part):
    return cache_entries(jax.random.fold_in(key, 303), PROMPTS, PLEN)


def draw_tail_cache(key, part):
    return cache_entries(jax.random.fold_in(key, 404), CONTS, TLEN)


def draw_q_gain(key, part):
    logs = jax.random.uniform(jax.random.fold_in(key, 505), (HD,), jnp.float32, math.log(0.5), math.log(2.0))
    gains = jnp.exp(logs)
    return gains.astype(jnp.float32)


def steps_of(stream_key, extent, cuts, smallest, largest):
    gain, own = 1.0, jax.random.fold_in(stream_key, 6)
    for axis_at, blocks in cuts:
        heights = jnp.exp(jax.random.uniform(jax.random.fold_in(own, axis_at), (blocks,), jnp.float32, smallest / len(cuts), largest / len(cuts)))
        gain = gain * jnp.repeat(heights, extent[axis_at] // blocks).reshape([-1 if axis == axis_at else 1 for axis in range(len(extent))])
    return gain


def gaussian(key, shape, width, bound, pieces=(), kind=jnp.bfloat16):
    gain = steps_of(key, shape, pieces, -0.22, 0.18) if pieces else 1.0
    array = jax.random.normal(key, shape, jnp.float32) * width * gain
    return jnp.minimum(jnp.maximum(array, -bound), bound).astype(kind)


def setup_inputs(seed: int = 0) -> dict:
    arg_keys = jax.random.split(jax.random.key(seed), 12)
    hidden_in = gaussian(arg_keys[0], (ROWS, D), 1.0, 6.0, ((0, 16),))
    attn_gain = jnp.clip(1.0 + 0.18 * jax.random.normal(arg_keys[1], (D,), jnp.float32), 0.1, 1.9)
    w_qkv = gaussian(arg_keys[2], (D, (HEADS + 2 * KVH) * HD), D ** -0.5, 0.125, ((0, 16), (1, 8)))
    q_gain = draw_q_gain(jax.random.fold_in(arg_keys[11], 71), 0)
    k_gain = jnp.clip(1.0 + 0.18 * jax.random.normal(arg_keys[4], (HD,), jnp.float32), 0.1, 1.9)
    w_out = gaussian(arg_keys[5], (HEADS * HD, D), (HEADS * HD) ** -0.5, 0.125, ((0, 8), (1, 16)))
    prefix_cache = draw_prefix_cache(jax.random.fold_in(arg_keys[11], 71), 0)
    tail_cache = draw_tail_cache(jax.random.fold_in(arg_keys[11], 71), 0)
    prompt_lens = draw_prompt_lens(jax.random.fold_in(arg_keys[11], 71), 0)
    tail_lens = draw_tail_lens(jax.random.fold_in(arg_keys[11], 71), 0)
    slot_prompt = jax.random.permutation(arg_keys[10], PROMPTS).astype(jnp.int32)
    return {"hidden_in": hidden_in, "attn_gain": attn_gain, "w_qkv": w_qkv, "q_gain": q_gain, "k_gain": k_gain, "w_out": w_out, "prefix_cache": prefix_cache, "tail_cache": tail_cache, "prompt_lens": prompt_lens, "tail_lens": tail_lens, "slot_prompt": slot_prompt}


epsilon = 1e-06
rope_base = 1000000.0
negative_fill = -1e+30

def rms_norm(values, norm_gain):
    mean_square = lax.optimization_barrier(jnp.mean(values * values, axis=-1, keepdims=True))
    return values * lax.rsqrt(mean_square + epsilon) * norm_gain

def rotate(values, position):
    half_width = values.shape[-1] // 2
    channel = jnp.arange(half_width, dtype=jnp.float32)
    inverse_freq = jnp.exp(channel * (-2.0 / values.shape[-1]) * math.log(rope_base))
    angles = position[..., None] * inverse_freq
    cosine = jnp.cos(angles)
    sines = jnp.sin(angles)
    leading = values[..., :half_width]
    trailing = values[..., half_width:]
    return jnp.concatenate([leading * cosine - trailing * sines, trailing * cosine + leading * sines], axis=-1)

def widen(values):
    return lax.optimization_barrier(values).astype(jnp.float32)

def combine_parts(prefix_out, prefix_lse, tail_out, tail_lse):
    highest = jnp.maximum(prefix_lse, tail_lse)
    prefix_share = jnp.exp(prefix_lse - highest)
    tail_share = jnp.exp(tail_lse - highest)
    merged = (prefix_share[..., None] * prefix_out + tail_share[..., None] * tail_out) / (prefix_share + tail_share)[..., None]
    return (merged.astype(jnp.bfloat16), highest + jnp.log(prefix_share + tail_share))

def reference(hidden_in, attn_gain, w_qkv, q_gain, k_gain, w_out, prefix_cache, tail_cache, prompt_lens, tail_lens, slot_prompt):
    group_size = HEADS // KVH
    per_prompt = CONT * NEW
    scaling = HD ** (-0.5)
    residual = hidden_in.astype(jnp.float32)
    normed = rms_norm(residual, attn_gain).astype(jnp.bfloat16)
    projected = jnp.dot(normed, w_qkv, preferred_element_type=jnp.float32).reshape(ROWS, KVH, group_size + 2, HD)
    row_index = jnp.arange(ROWS, dtype=jnp.int32)
    continuation = row_index // NEW
    prompt_index = continuation // CONT
    step_index = row_index % NEW
    position = (prompt_lens[prompt_index] + tail_lens[continuation] + step_index).astype(jnp.float32)
    queries = rotate(rms_norm(projected[:, :, :group_size], q_gain), position[:, None, None]).astype(jnp.bfloat16)
    new_keys = rotate(rms_norm(projected[:, :, group_size], k_gain), position[:, None]).astype(jnp.bfloat16)
    new_values = projected[:, :, group_size + 1].astype(jnp.bfloat16)
    new_cache = jnp.stack([new_keys.reshape(ROWS, KVH * HD), new_values.reshape(ROWS, KVH * HD)])
    inverse = jnp.zeros((PROMPTS,), jnp.int32).at[slot_prompt].set(jnp.arange(PROMPTS, dtype=jnp.int32))
    causal = jnp.arange(NEW)[None, :] <= jnp.arange(NEW)[:, None]

    def one_prompt(prompt_number):
        slot_number = inverse[prompt_number]
        row_begin = (prompt_number * per_prompt).astype(jnp.int32)
        query_rows = widen(lax.dynamic_slice_in_dim(queries, row_begin, per_prompt, 0))
        prefix_keys = lax.dynamic_index_in_dim(prefix_cache[0], slot_number, 0, keepdims=False).reshape(PLEN, KVH, HD).astype(jnp.float32)
        prefix_values = lax.dynamic_index_in_dim(prefix_cache[1], slot_number, 0, keepdims=False).reshape(PLEN, KVH, HD).astype(jnp.float32)
        prefix_scores = jnp.einsum('rghd,kgd->rghk', query_rows, prefix_keys) * scaling
        alive = jnp.arange(PLEN, dtype=jnp.int32) < prompt_lens[prompt_number]
        prefix_scores = jnp.where(alive, prefix_scores, negative_fill)
        prefix_max = lax.optimization_barrier(jnp.max(prefix_scores, axis=-1))
        prefix_weights = jnp.exp(prefix_scores - prefix_max[..., None])
        prefix_total = lax.optimization_barrier(jnp.sum(prefix_weights, axis=-1))
        prefix_num = jnp.einsum('rghk,kgd->rghd', widen(prefix_weights.astype(jnp.bfloat16)), prefix_values)
        prefix_out = prefix_num / prefix_total[..., None]
        prefix_lse = prefix_max + jnp.log(prefix_total)
        cont_begin = (prompt_number * CONT).astype(jnp.int32)
        tail_query = query_rows.reshape(CONT, NEW, KVH, group_size, HD)
        tail_keys = lax.dynamic_slice_in_dim(tail_cache[0], cont_begin, CONT, 0).reshape(CONT, TLEN, KVH, HD).astype(jnp.float32)
        tail_values = lax.dynamic_slice_in_dim(tail_cache[1], cont_begin, CONT, 0).reshape(CONT, TLEN, KVH, HD).astype(jnp.float32)
        tail_length = lax.dynamic_slice_in_dim(tail_lens, cont_begin, CONT, 0)
        own_keys = widen(lax.dynamic_slice_in_dim(new_keys, row_begin, per_prompt, 0)).reshape(CONT, NEW, KVH, HD)
        own_values = widen(lax.dynamic_slice_in_dim(new_values, row_begin, per_prompt, 0)).reshape(CONT, NEW, KVH, HD)
        cached_scores = jnp.einsum('ctghd,csgd->ctghs', tail_query, tail_keys) * scaling
        cached_alive = jnp.arange(TLEN, dtype=jnp.int32)[None, :] < tail_length[:, None]
        cached_scores = jnp.where(cached_alive[:, None, None, None, :], cached_scores, negative_fill)
        own_scores = jnp.einsum('ctghd,cugd->ctghu', tail_query, own_keys) * scaling
        own_scores = jnp.where(causal[None, :, None, None, :], own_scores, negative_fill)
        tail_max = jnp.maximum(lax.optimization_barrier(jnp.max(cached_scores, axis=-1)), lax.optimization_barrier(jnp.max(own_scores, axis=-1)))
        cached_weights = jnp.exp(cached_scores - tail_max[..., None])
        own_weights = jnp.exp(own_scores - tail_max[..., None])
        tail_total = lax.optimization_barrier(jnp.sum(cached_weights, axis=-1)) + lax.optimization_barrier(jnp.sum(own_weights, axis=-1))
        tail_num = jnp.einsum('ctghs,csgd->ctghd', widen(cached_weights.astype(jnp.bfloat16)), tail_values)
        tail_num = tail_num + jnp.einsum('ctghu,cugd->ctghd', widen(own_weights.astype(jnp.bfloat16)), own_values)
        tail_out = (tail_num / tail_total[..., None]).reshape(per_prompt, KVH, group_size, HD)
        tail_lse = (tail_max + jnp.log(tail_total)).reshape(per_prompt, KVH, group_size)
        return combine_parts(prefix_out, prefix_lse, tail_out, tail_lse)
    attention, scores = lax.map(one_prompt, jnp.arange(PROMPTS, dtype=jnp.int32))
    attention = attention.reshape(ROWS, HEADS * HD)
    scores = scores.reshape(ROWS, HEADS)
    hidden_out = (residual + jnp.dot(attention, w_out, preferred_element_type=jnp.float32)).astype(jnp.bfloat16)
    return (hidden_out, scores, new_cache)
```

```python
import math

import jax
import jax.numpy as jnp
from jax import lax
from jax.experimental import pallas as pl
from jax.experimental.pallas import tpu as pltpu
from jax.sharding import PartitionSpec as P

HD = 128
ROWS = 128
PER = 32
PLEN = 4096
TLEN = 256
KB = 1024
MSG = 80
EPS = 1e-06
NEG = -1e30
SCALE = HD ** (-0.5)
LOG2E = 1.4426950408889634
F32 = jnp.float32
BF16 = jnp.bfloat16
AXES = ("wide", "narrow")
SMEM = pltpu.SMEM


def device(z, y, x, core):
    return ((z % 4) * 4 + y % 4) * 8 + (x % 4) * 2 + core


def ring(first, step):
    pairs = []
    for z in range(4):
        for y in range(4):
            for x in range(4):
                for core in range(2):
                    along_y = (core == 0) == first
                    target = device(z, y + step, x, core) if along_y else device(z + step, y, x, core)
                    pairs.append((device(z, y, x, core), target))
    return pairs


def shift(value, first, step):
    return lax.ppermute(value, AXES, ring(first, step))


def shift_x(value, step):
    return lax.ppermute(value, "narrow", [(n, (n + 2 * step) % 8) for n in range(8)])


def swap_core(value):
    return lax.ppermute(value, "narrow", [(n, n ^ 1) for n in range(8)])


def call(kernel, out_shape, args, smem=(), anys=(), scratch=(), cost=None):
    specs = []
    for i in range(len(args)):
        if i in smem:
            specs.append(pl.BlockSpec(memory_space=SMEM))
        elif i in anys:
            specs.append(pl.BlockSpec(memory_space=pl.ANY))
        else:
            specs.append(pl.BlockSpec(memory_space=pltpu.VMEM))
    single = not isinstance(out_shape, (tuple, list))
    outs = pl.BlockSpec(memory_space=pltpu.VMEM)
    if not single:
        outs = [pl.BlockSpec(memory_space=pltpu.VMEM)] * len(out_shape)
    flops, nbytes = cost or (1 << 20, 1 << 20)
    return pl.pallas_call(
        kernel,
        out_shape=out_shape,
        in_specs=specs,
        out_specs=outs,
        scratch_shapes=list(scratch),
        compiler_params=pltpu.CompilerParams(vmem_limit_bytes=40 << 20),
        cost_estimate=pl.CostEstimate(flops=flops, bytes_accessed=nbytes, transcendentals=0),
    )(*args)


def struct(shape, dtype):
    return jax.ShapeDtypeStruct(shape, dtype)


def norm_kernel(ids, hidden, gain, *outs):
    values = hidden[...].astype(F32)
    mean_square = jnp.mean(values * values, axis=-1, keepdims=True)
    factor = lax.rsqrt(mean_square + EPS)
    b, core = ids[1], ids[2]
    for block in range(16):
        fz, fy = block // 4, block % 4
        part = hidden[:, block * HD : (block + 1) * HD].astype(F32) * factor
        part = (part * gain[:, block * HD : (block + 1) * HD]).astype(BF16)
        fa = jnp.where(core == 0, fy, fz)
        fb = jnp.where(core == 0, fz, fy)
        target = lax.rem(fb - b + 4, 4)
        for d in range(4):

            @pl.when(target == d)
            def _():
                outs[d][fa] = part


def project_kernel(ids, *refs):
    acts, weights, outs = refs[:4], refs[4:8], refs[8:]
    a = ids[0]
    weight = jnp.concatenate([weights[e][...] for e in range(4)], axis=0)
    order = [lax.rem(a - e + 4, 4) for e in range(4)]
    for d in range(4):
        act = jnp.concatenate([acts[d][order[e]] for e in range(4)], axis=1)
        product = jnp.dot(act, weight, preferred_element_type=F32)
        outs[d][...] = product[:, : 2 * HD]
        outs[4 + d][...] = product[:, 2 * HD :]


def head_norm(values, gain, cosine, sine):
    mean_square = jnp.mean(values * values, axis=-1, keepdims=True)
    values = values * lax.rsqrt(mean_square + EPS) * gain
    return values * cosine + pltpu.roll(values, HD // 2, 1) * sine


def query_kernel(p0, p1, p2, p3, gain, cosine, sine, out):
    total = (p0[...] + p1[...]) + (p2[...] + p3[...])
    for h in range(2):
        head = head_norm(total[:, h * HD : (h + 1) * HD], gain[...], cosine[...], sine[...])
        head = head.astype(BF16)
        for j in range(4):
            out[j, h * PER : (h + 1) * PER] = head[j * PER : (j + 1) * PER]


def route_kernel(index, x0, x1, x2, x3, o0, o1, o2, o3, held):
    for d, ref in enumerate((x0, x1, x2, x3)):
        held[4 * d : 4 * d + 4] = ref[...]
    for e, ref in enumerate((o0, o1, o2, o3)):
        for k in range(4):
            ref[k] = held[index[4 * e + k]]


def column(rows, count):
    lane = lax.broadcasted_iota(jnp.int32, (count, HD), 1)
    row = lax.broadcasted_iota(jnp.int32, (count, HD), 0)
    spread = jnp.broadcast_to(rows, (count, HD))
    return jnp.sum(jnp.where(lane == row, spread, 0.0), axis=1, keepdims=True)


def tail_kernel(
    lens, p0, p1, p2, p3, queries, gain, cosine, sine, cache,
    new_cache, out, lse, keys, values, sems,
):
    groups = 8
    conts = 8

    def fetch(which, g, target):
        return pltpu.make_async_copy(
            cache.at[which, pl.ds(g * conts, conts)], target.at[g], sems.at[which, g]
        )

    for g in range(groups):
        fetch(0, g, keys).start()
        fetch(1, g, values).start()
    total = (p0[...] + p1[...]) + (p2[...] + p3[...])
    new_cache[0] = head_norm(total[:, :HD], gain[...], cosine[...], sine[...]).astype(BF16)
    new_cache[1] = total[:, HD:].astype(BF16)
    row = lax.broadcasted_iota(jnp.int32, (32, TLEN), 0)
    lane = lax.broadcasted_iota(jnp.int32, (32, TLEN), 1)
    owner = lax.rem(row, 16) // 2
    small_row = lax.broadcasted_iota(jnp.int32, (32, 16), 0)
    small_col = lax.broadcasted_iota(jnp.int32, (32, 16), 1)
    visible = (lax.rem(small_row, 16) // 2 == small_col // 2) & (
        lax.rem(small_col, 2) <= lax.rem(small_row, 2)
    )
    owner_out = lax.rem(lax.broadcasted_iota(jnp.int32, (32, HD), 0), 16) // 2
    contract = (((1,), (1,)), ((), ()))
    for g in range(groups):
        j, half = g // 2, (g % 2) * 16
        q = jnp.concatenate(
            [queries[j, half : half + 16], queries[j, PER + half : PER + half + 16]], axis=0
        )
        fetch(0, g, keys).wait()
        score = jnp.zeros((32, TLEN), F32)
        length = jnp.zeros((32, TLEN), jnp.int32)
        for i in range(conts):
            part = lax.dot_general(q, keys[g, i], contract, preferred_element_type=F32)
            score = jnp.where(owner == i, part, score)
            length = jnp.where(owner == i, lens[g * conts + i], length)
        score = jnp.where(lane < length, score, NEG)
        fresh = lax.dot_general(
            q, new_cache[0, g * 16 : g * 16 + 16], contract, preferred_element_type=F32
        )
        fresh = jnp.where(visible, fresh, NEG)
        high = jnp.maximum(
            jnp.max(score, axis=1, keepdims=True), jnp.max(fresh, axis=1, keepdims=True)
        )
        weight = jnp.exp2((score - high) * (SCALE * LOG2E))
        fresh_weight = jnp.exp2((fresh - high) * (SCALE * LOG2E))
        sums = jnp.sum(weight, axis=1, keepdims=True) + jnp.sum(
            fresh_weight, axis=1, keepdims=True
        )
        weight = weight.astype(BF16)
        fetch(1, g, values).wait()
        acc = jnp.zeros((32, HD), F32)
        for i in range(conts):
            part = jnp.dot(weight, values[g, i], preferred_element_type=F32)
            acc = jnp.where(owner_out == i, part, acc)
        acc = acc + jnp.dot(
            fresh_weight.astype(BF16),
            new_cache[1, g * 16 : g * 16 + 16],
            preferred_element_type=F32,
        )
        acc = acc / sums
        logs = jnp.broadcast_to(high * SCALE + jnp.log(sums), (32, HD))
        for h in range(2):
            out[h, g * 16 : g * 16 + 16] = acc[h * 16 : h * 16 + 16]
            lse[h, g * 16 : g * 16 + 16] = logs[h * 16 : h * 16 + 16]


def prefix_kernel(select, lens, r0, r1, r2, r3, cache, out, held, keys, values, scores, sems):
    blocks = PLEN // KB

    def fetch(which, s, i, target):
        return pltpu.make_async_copy(
            cache.at[which, s, pl.ds(i * KB, KB)], target.at[s, i], sems.at[which, s, i]
        )

    counts = [(lens[s] + (KB - 1)) // KB for s in range(4)]
    for s in range(4):
        for i in range(blocks):

            @pl.when(i < counts[s])
            def _():
                fetch(0, s, i, keys).start()
                fetch(1, s, i, values).start()

    for e, ref in enumerate((r0, r1, r2, r3)):
        held[e] = ref[...]
    lane = lax.broadcasted_iota(jnp.int32, (64, KB), 1)
    contract = (((1,), (1,)), ((), ()))
    for s in range(4):
        q = held[select[s], s]

        def first(i, high):
            fetch(0, s, i, keys).wait()
            part = lax.dot_general(q, keys[s, i], contract, preferred_element_type=F32)
            part = jnp.where(lane < lens[s] - i * KB, part, NEG)
            scores[i] = part
            for c in range(KB // HD):
                high = jnp.maximum(high, part[:, c * HD : (c + 1) * HD])
            return high

        high = lax.fori_loop(0, counts[s], first, jnp.full((64, HD), NEG, F32))
        high = jnp.max(high, axis=1, keepdims=True)

        def second(i, carry):
            sums, acc = carry
            weight = jnp.exp2((scores[i] - high) * (SCALE * LOG2E))
            for c in range(KB // HD):
                sums = sums + weight[:, c * HD : (c + 1) * HD]
            fetch(1, s, i, values).wait()
            acc = acc + jnp.dot(weight.astype(BF16), values[s, i], preferred_element_type=F32)
            return sums, acc

        zero = jnp.zeros((64, HD), F32)
        sums, acc = lax.fori_loop(0, counts[s], second, (zero, zero))
        sums = jnp.sum(sums, axis=1, keepdims=True)
        out[s, :64] = (acc / sums).astype(BF16)
        logs = jnp.broadcast_to(high * SCALE + jnp.log(sums), (64, HD))
        row = lax.broadcasted_iota(jnp.int32, (64, HD), 0)
        column_of = lax.broadcasted_iota(jnp.int32, (64, HD), 1)
        line = jnp.sum(jnp.where(row == column_of, logs, 0.0), axis=0, keepdims=True)
        top = line.astype(BF16).astype(F32)
        middle = (line - top).astype(BF16).astype(F32)
        low = line - top - middle
        which = lax.broadcasted_iota(jnp.int32, (16, HD), 0)
        lines = jnp.where(
            which == 0, top, jnp.where(which == 1, middle, jnp.where(which == 2, low, 0.0))
        )
        out[s, 64:MSG] = lines.astype(BF16)


def finish_kernel(
    ids, select, c0, c1, c2, c3, tail_out, tail_lse, w0, w1, w2, w3,
    scores, keep, send, held, attention,
):
    for e, ref in enumerate((c0, c1, c2, c3)):
        held[e] = ref[...]
    for j in range(4):
        message = held[select[j], j]
        lines = message[64:MSG].astype(F32)
        line = (lines[0:1] + lines[1:2]) + lines[2:3]
        logs = column(line, 64)
        for h in range(2):
            rows = slice(j * PER, (j + 1) * PER)
            prefix_out = message[h * PER : (h + 1) * PER].astype(F32)
            prefix_lse = logs[h * PER : (h + 1) * PER]
            own_lse = tail_lse[h, rows][:, 0:1]
            high = jnp.maximum(prefix_lse, own_lse)
            share_a = jnp.exp(prefix_lse - high)
            share_b = jnp.exp(own_lse - high)
            both = share_a + share_b
            merged = (share_a * prefix_out + share_b * tail_out[h, rows]) / both
            attention[rows, h * HD : (h + 1) * HD] = merged.astype(BF16)
            scores[rows, h : h + 1] = high + jnp.log(both)
    a, b, core, x = ids[0], ids[1], ids[2], ids[3]
    left = attention[...]
    for e, ref in enumerate((w0, w1, w2, w3)):
        for d in range(4):
            product = jnp.dot(left, ref[d], preferred_element_type=F32)
            at_a, at_b = lax.rem(a - d + 4, 4), lax.rem(b - e + 4, 4)
            block = jnp.where(core == 0, 4 * at_b + at_a, 4 * at_a + at_b)
            mine = (block // 8) == core
            pair = lax.rem(block, 8) // 2
            side = lax.rem(block, 2)

            @pl.when(mine)
            def _():
                keep[lax.rem(pair - x + 4, 4), side] = product

            @pl.when(jnp.logical_not(mine))
            def _():
                send[pair, side] = product.astype(BF16)


def first_sum_kernel(ids, keep, got, o0, o1, o2, o3):
    x = ids[3]
    for d in range(4):
        total = keep[d] + got[lax.rem(x + d, 4)].astype(F32)
        if d == 0:
            o0[...] = total
        else:
            (o1, o2, o3)[d - 1][...] = total.astype(BF16)


def second_sum_kernel(ids, o0, g1, g2, g3, hidden, out):
    core, x = ids[2], ids[3]
    for side in range(2):
        total = o0[side] + (
            g1[side].astype(F32) + g2[side].astype(F32) + g3[side].astype(F32)
        )
        at = pl.multiple_of((core * 8 + x * 2 + side) * HD, HD)
        out[side] = (hidden[:, pl.ds(at, HD)].astype(F32) + total).astype(BF16)


def gather_kernel(ids, mine, other, out):
    core, x = ids[2], ids[3]
    for d in range(4):
        for side in range(2):
            at = lax.rem(x - d + 4, 4) * 2 + side
            out[:, pl.ds(pl.multiple_of((core * 8 + at) * HD, HD), HD)] = mine[d, side]
            out[:, pl.ds(pl.multiple_of(((1 - core) * 8 + at) * HD, HD), HD)] = other[d, side]


def lookup(indices, table):
    entries = jnp.arange(table.shape[0], dtype=jnp.int32)
    return jnp.sum(jnp.where(indices[:, None] == entries[None, :], table[None, :], 0), axis=1)


def split(wide, core):
    z, y = wide // 4, wide % 4
    return jnp.where(core == 0, y, z), jnp.where(core == 0, z, y)


def routing(source, a, b, core):
    step = jnp.arange(16, dtype=jnp.int32) // 4
    at_b = (b + step) % 4
    wide = jnp.where(core == 0, 4 * at_b + a, 4 * a + at_b)
    wanted = lookup(wide * 4 + jnp.arange(16, dtype=jnp.int32) % 4, source)
    from_a, from_b = split(wanted // 4, core)
    index = ((a - from_a) % 4) * 4 + wanted % 4
    sender = (b - from_b[:4]) % 4
    return index, sender, wanted[:4]


def gather_ring(value, first):
    return [value] + [shift(value, first, step) for step in (1, 2, 3)]


def route(values, index, rows):
    held = gather_ring(values, True)
    shape = struct((4, rows, HD), BF16)
    sends = call(
        route_kernel,
        [shape] * 4,
        [index] + held,
        smem=(0,),
        scratch=[pltpu.VMEM((16, rows, HD), BF16)],
    )
    return [sends[0]] + [shift(sends[step], False, step) for step in (1, 2, 3)]


def body(
    hidden_in, attn_gain, w_qkv, q_gain, k_gain, w_out,
    prefix_cache, tail_cache, prompt_lens, tail_lens, slot_prompt,
):
    wide = lax.axis_index("wide").astype(jnp.int32)
    narrow = lax.axis_index("narrow").astype(jnp.int32)
    core, x = narrow % 2, narrow // 2
    a, b = split(wide, core)
    ids = jnp.stack([a, b, core, x]).astype(jnp.int32)

    everyone = jnp.arange(64, dtype=jnp.int32)
    inverse = jnp.sum(
        jnp.where(slot_prompt[:, None] == everyone[None, :], everyone[:, None], 0), axis=0
    )
    ask_index, ask_sender, owners = routing(slot_prompt, a, b, core)
    home_index, home_sender, _ = routing(inverse, a, b, core)
    slot_lens = lookup(owners, prompt_lens)
    row = jnp.arange(ROWS, dtype=jnp.int32)
    position = (
        lookup(wide * 4 + row // PER, prompt_lens) + lookup(row // 2, tail_lens) + row % 2
    ).astype(F32)
    channel = jnp.arange(HD // 2, dtype=F32)
    inverse_freq = jnp.exp(channel * (-2.0 / HD) * math.log(1000000.0))
    angles = position[:, None] * inverse_freq
    cosine, sine = jnp.cos(angles), jnp.sin(angles)
    cosine = jnp.concatenate([cosine, cosine], axis=1)
    sine = jnp.concatenate([-sine, sine], axis=1)
    q_gain, k_gain = q_gain.reshape(1, HD), k_gain.reshape(1, HD)

    weights = gather_ring(w_qkv, True)
    shape = struct((4, ROWS, HD), BF16)
    acts = call(norm_kernel, [shape] * 4, [ids, hidden_in, attn_gain.reshape(1, -1)], smem=(0,))
    acts = [acts[0]] + [shift(acts[step], False, step) for step in (1, 2, 3)]
    partial = struct((ROWS, 2 * HD), F32)
    parts = call(
        project_kernel,
        [partial] * 8,
        [ids] + acts + weights,
        smem=(0,),
        cost=(2 * 512 * 512 * 512, 3 << 20),
    )
    query_parts = [parts[0]] + [shift(parts[step], False, 4 - step) for step in (1, 2, 3)]
    pair_parts = [parts[4]] + [shift(parts[4 + step], False, 4 - step) for step in (1, 2, 3)]
    queries = call(
        query_kernel, struct((4, 64, HD), BF16), query_parts + [q_gain, cosine, sine]
    )

    asked = route(queries, ask_index, 64)

    new_cache, tail_out, tail_lse = call(
        tail_kernel,
        [
            struct((2, ROWS, HD), BF16),
            struct((2, ROWS, HD), F32),
            struct((2, ROWS, HD), F32),
        ],
        [tail_lens] + pair_parts + [queries, k_gain, cosine, sine, tail_cache],
        smem=(0,),
        anys=(9,),
        scratch=[
            pltpu.VMEM((8, 8, TLEN, HD), BF16),
            pltpu.VMEM((8, 8, TLEN, HD), BF16),
            pltpu.SemaphoreType.DMA((2, 8)),
        ],
        cost=(2 * 2 * 64 * 32 * TLEN * HD, 8 << 20),
    )

    results = call(
        prefix_kernel,
        struct((4, MSG, HD), BF16),
        [ask_sender, slot_lens] + asked + [prefix_cache],
        smem=(0, 1),
        anys=(6,),
        scratch=[
            pltpu.VMEM((4, 4, 64, HD), BF16),
            pltpu.VMEM((4, PLEN // KB, KB, HD), BF16),
            pltpu.VMEM((4, PLEN // KB, KB, HD), BF16),
            pltpu.VMEM((PLEN // KB, 64, KB), F32),
            pltpu.SemaphoreType.DMA((2, 4, PLEN // KB)),
        ],
        cost=(2 * 2 * 4 * 64 * PLEN * HD, 8 << 20),
    )
    homes = route(results, home_index, MSG)

    near = jnp.stack(gather_ring(w_out, True))
    far = gather_ring(near, False)

    scores, keep, send = call(
        finish_kernel,
        [
            struct((ROWS, 2), F32),
            struct((4, 2, ROWS, HD), F32),
            struct((4, 2, ROWS, HD), BF16),
        ],
        [ids, home_sender] + homes + [tail_out, tail_lse] + far,
        smem=(0, 1),
        scratch=[pltpu.VMEM((4, 4, MSG, HD), BF16), pltpu.VMEM((ROWS, 2 * HD), BF16)],
        cost=(2 * ROWS * 256 * 2048, 3 << 20),
    )
    got = swap_core(send)
    block = struct((2, ROWS, HD), BF16)
    sums = call(
        first_sum_kernel,
        [struct((2, ROWS, HD), F32), block, block, block],
        [ids, keep, got],
        smem=(0,),
    )
    moved = [shift_x(sums[step], step) for step in (1, 2, 3)]
    mine = call(second_sum_kernel, block, [ids, sums[0]] + moved + [hidden_in], smem=(0,))
    ours = jnp.stack([mine] + [shift_x(mine, step) for step in (1, 2, 3)])
    theirs = swap_core(ours)
    hidden_out = call(
        gather_kernel, struct((ROWS, 2048), BF16), [ids, ours, theirs], smem=(0,)
    )
    return (hidden_out, scores, new_cache)


def solution(mesh):
    in_specs = (
        P("wide", None),
        P(),
        P("wide", "narrow"),
        P(),
        P(),
        P("narrow", "wide"),
        P(None, "wide", None, "narrow"),
        P(None, "wide", None, "narrow"),
        P(),
        P("wide"),
        P(),
    )
    out_specs = (P("wide", None), P("wide", "narrow"), P(None, "wide", "narrow"))
    return jax.shard_map(body, mesh=mesh, in_specs=in_specs, out_specs=out_specs, check_vma=False)
```

```python
import functools
import math

import jax
import jax.numpy as jnp
from jax import lax
from jax.experimental import pallas as pl
from jax.experimental.pallas import tpu as pltpu
from jax.sharding import PartitionSpec as P

HD = 128
ROWS = 128
PER = 32
PLEN = 4096
TLEN = 256
KB = 1024
MSG = 80
EPS = 1e-06
NEG = -1e30
HINT = 1 << 34
SCALE = HD ** (-0.5)
LOG2E = 1.4426950408889634
F32 = jnp.float32
BF16 = jnp.bfloat16
AXES = ("wide", "narrow")
SMEM = pltpu.SMEM


def device(z, y, x, core):
    return ((z % 4) * 4 + y % 4) * 8 + (x % 4) * 2 + core


def ring(first, step):
    pairs = []
    for z in range(4):
        for y in range(4):
            for x in range(4):
                for core in range(2):
                    along_y = (core == 0) == first
                    target = device(z, y + step, x, core) if along_y else device(z + step, y, x, core)
                    pairs.append((device(z, y, x, core), target))
    return pairs


def shift(value, first, step):
    return lax.ppermute(value, AXES, ring(first, step))


def shift_x(value, step):
    return lax.ppermute(value, "narrow", [(n, (n + 2 * step) % 8) for n in range(8)])


def swap_core(value):
    return lax.ppermute(value, "narrow", [(n, n ^ 1) for n in range(8)])


def call(kernel, out_shape, args, smem=(), smem_out=(), scratch=(), cost=None):
    def spec(is_scalar):
        return pl.BlockSpec(memory_space=SMEM if is_scalar else pltpu.VMEM)

    specs = [spec(i in smem) for i in range(len(args))]
    if isinstance(out_shape, (tuple, list)):
        outs = [spec(i in smem_out) for i in range(len(out_shape))]
    else:
        outs = spec(False)
    flops, nbytes = cost or (1 << 20, 1 << 20)
    return pl.pallas_call(
        kernel,
        out_shape=out_shape,
        in_specs=specs,
        out_specs=outs,
        scratch_shapes=list(scratch),
        compiler_params=pltpu.CompilerParams(vmem_limit_bytes=8 << 20),
        cost_estimate=pl.CostEstimate(flops=flops, bytes_accessed=nbytes, transcendentals=0),
    )(*args)


def struct(shape, dtype):
    return jax.ShapeDtypeStruct(shape, dtype)


def tables_kernel(ids, prompts, lens, tails, freq, table, angles, inverse):
    a, b, core = ids[0], ids[1], ids[2]
    wide = jnp.where(core == 0, 4 * b + a, 4 * a + b)

    def invert(i, carry):
        inverse[prompts[i]] = i
        return carry

    lax.fori_loop(0, 64, invert, 0, unroll=True)
    for base, source in ((0, prompts), (24, inverse)):
        for e in range(4):
            at_b = lax.rem(b + e, 4)
            there = jnp.where(core == 0, 4 * at_b + a, 4 * a + at_b)
            for k in range(4):
                item = source[there * 4 + k]
                z, y = item // 16, lax.rem(item // 4, 4)
                from_a, from_b = jnp.where(core == 0, y, z), jnp.where(core == 0, z, y)
                table[base + 4 * e + k] = lax.rem(a - from_a + 4, 4) * 4 + lax.rem(item, 4)
                if e == 0:
                    table[base + 16 + k] = lax.rem(b - from_b + 4, 4)
                    table[base + 20 + k] = lens[item]
    row = lax.broadcasted_iota(jnp.int32, (ROWS, HD), 0)
    pair = row // 2
    position = jnp.zeros((ROWS, HD), jnp.int32)
    for c in range(64):
        position = jnp.where(pair == c, lens[wide * 4 + c // 16] + tails[c], position)
    position = position + lax.rem(row, 2)
    angles[...] = position.astype(F32) * freq[...]


def norm_kernel(hidden, gain, out):
    values = hidden[...].astype(F32)
    mean_square = jnp.mean(values * values, axis=-1, keepdims=True)
    factor = lax.rsqrt(mean_square + EPS)
    for block in range(16):
        part = hidden[:, block * HD : (block + 1) * HD].astype(F32) * factor
        out[block] = (part * gain[:, block * HD : (block + 1) * HD]).astype(BF16)


def pack_kernel(w0, w1, w2, w3, first, second):
    for d, ref in enumerate((w0, w1, w2, w3)):
        first[d] = ref[:, : 2 * HD]
        second[d] = ref[:, 2 * HD :]


def project(ids, normed, refs):
    a, b, core = ids[0], ids[1], ids[2]
    total = jnp.zeros((ROWS, 2 * HD), F32)
    for e in range(4):
        at_b = lax.rem(b - e + 4, 4)
        left = []
        for d in range(4):
            at_a = lax.rem(a - d + 4, 4)
            left.append(normed[jnp.where(core == 0, 4 * at_b + at_a, 4 * at_a + at_b)])
        right = jnp.concatenate([refs[e][d, :, : 2 * HD] for d in range(4)], axis=0)
        total = total + jnp.dot(
            jnp.concatenate(left, axis=1), right, preferred_element_type=F32
        )
    return total


def head_norm(values, gain, cosine, sine):
    mean_square = jnp.mean(values * values, axis=-1, keepdims=True)
    values = values * lax.rsqrt(mean_square + EPS) * gain
    return values * cosine + pltpu.roll(values, HD // 2, 1) * sine


def query_kernel(ids, normed, w0, w1, w2, w3, gain, cosine, sine, out):
    total = project(ids, normed, (w0, w1, w2, w3))
    for h in range(2):
        head = head_norm(total[:, h * HD : (h + 1) * HD], gain[...], cosine[...], sine[...])
        head = head.astype(BF16)
        for j in range(4):
            out[j, h * PER : (h + 1) * PER] = head[j * PER : (j + 1) * PER]


def pair_kernel(ids, normed, w0, w1, w2, w3, gain, cosine, sine, out):
    total = project(ids, normed, (w0, w1, w2, w3))
    out[0] = head_norm(total[:, :HD], gain[...], cosine[...], sine[...]).astype(BF16)
    out[1] = total[:, HD:].astype(BF16)


def route_kernel(base, index, x0, x1, x2, x3, o0, o1, o2, o3, held):
    for d, ref in enumerate((x0, x1, x2, x3)):
        held[4 * d : 4 * d + 4] = ref[...]
    for e, ref in enumerate((o0, o1, o2, o3)):
        for k in range(4):
            ref[k] = held[index[base + 4 * e + k]]


def column(rows, count):
    lane = lax.broadcasted_iota(jnp.int32, (count, HD), 1)
    row = lax.broadcasted_iota(jnp.int32, (count, HD), 0)
    spread = jnp.broadcast_to(rows, (count, HD))
    return jnp.sum(jnp.where(lane == row, spread, 0.0), axis=1, keepdims=True)


def tail_kernel(start, lens, queries, new_cache, cache, out, lse):
    conts = 8
    row = lax.broadcasted_iota(jnp.int32, (32, TLEN), 0)
    lane = lax.broadcasted_iota(jnp.int32, (32, TLEN), 1)
    owner = lax.rem(row, 16) // 2
    small_row = lax.broadcasted_iota(jnp.int32, (32, 16), 0)
    small_col = lax.broadcasted_iota(jnp.int32, (32, 16), 1)
    visible = (lax.rem(small_row, 16) // 2 == small_col // 2) & (
        lax.rem(small_col, 2) <= lax.rem(small_row, 2)
    )
    owner_out = lax.rem(lax.broadcasted_iota(jnp.int32, (32, HD), 0), 16) // 2
    contract = (((1,), (1,)), ((), ()))
    for g in range(start, start + 4):
        j, half = g // 2, (g % 2) * 16
        q = jnp.concatenate(
            [queries[j, half : half + 16], queries[j, PER + half : PER + half + 16]], axis=0
        )
        score = jnp.zeros((32, TLEN), F32)
        length = jnp.zeros((32, TLEN), jnp.int32)
        for i in range(conts):
            part = lax.dot_general(q, cache[0, g * conts + i], contract, preferred_element_type=F32)
            score = jnp.where(owner == i, part, score)
            length = jnp.where(owner == i, lens[g * conts + i], length)
        score = jnp.where(lane < length, score, NEG)
        fresh = lax.dot_general(
            q, new_cache[0, g * 16 : g * 16 + 16], contract, preferred_element_type=F32
        )
        fresh = jnp.where(visible, fresh, NEG)
        high = jnp.maximum(
            jnp.max(score, axis=1, keepdims=True), jnp.max(fresh, axis=1, keepdims=True)
        )
        weight = jnp.exp2((score - high) * (SCALE * LOG2E))
        fresh_weight = jnp.exp2((fresh - high) * (SCALE * LOG2E))
        sums = jnp.sum(weight, axis=1, keepdims=True) + jnp.sum(
            fresh_weight, axis=1, keepdims=True
        )
        weight = weight.astype(BF16)
        acc = jnp.zeros((32, HD), F32)
        for i in range(conts):
            part = jnp.dot(weight, cache[1, g * conts + i], preferred_element_type=F32)
            acc = jnp.where(owner_out == i, part, acc)
        acc = acc + jnp.dot(
            fresh_weight.astype(BF16),
            new_cache[1, g * 16 : g * 16 + 16],
            preferred_element_type=F32,
        )
        acc = acc / sums
        logs = jnp.broadcast_to(high * SCALE + jnp.log(sums), (32, HD))
        for h in range(2):
            at = (g - start) * 16
            out[h, at : at + 16] = acc[h * 16 : h * 16 + 16]
            lse[h, at : at + 16] = logs[h * 16 : h * 16 + 16]


def prefix_kernel(table, r0, r1, r2, r3, cache, out, held, scores):
    select = [table[16 + s] for s in range(4)]
    lens = [table[20 + s] for s in range(4)]
    counts = [(lens[s] + (KB - 1)) // KB for s in range(4)]
    for e, ref in enumerate((r0, r1, r2, r3)):
        held[e] = ref[...]
    lane = lax.broadcasted_iota(jnp.int32, (64, KB), 1)
    contract = (((1,), (1,)), ((), ()))
    for s in range(4):
        q = held[select[s], s]

        def first(i, high):
            block = cache[0, s, pl.ds(pl.multiple_of(i * KB, KB), KB)]
            part = lax.dot_general(q, block, contract, preferred_element_type=F32)
            part = jnp.where(lane < lens[s] - i * KB, part, NEG)
            scores[i] = part
            for c in range(KB // HD):
                high = jnp.maximum(high, part[:, c * HD : (c + 1) * HD])
            return high

        high = lax.fori_loop(0, counts[s], first, jnp.full((64, HD), NEG, F32))
        high = jnp.max(high, axis=1, keepdims=True)

        def second(i, carry):
            sums, acc = carry
            weight = jnp.exp2((scores[i] - high) * (SCALE * LOG2E))
            for c in range(KB // HD):
                sums = sums + weight[:, c * HD : (c + 1) * HD]
            block = cache[1, s, pl.ds(pl.multiple_of(i * KB, KB), KB)]
            acc = acc + jnp.dot(weight.astype(BF16), block, preferred_element_type=F32)
            return sums, acc

        zero = jnp.zeros((64, HD), F32)
        sums, acc = lax.fori_loop(0, counts[s], second, (zero, zero))
        sums = jnp.sum(sums, axis=1, keepdims=True)
        out[s, :64] = (acc / sums).astype(BF16)
        logs = jnp.broadcast_to(high * SCALE + jnp.log(sums), (64, HD))
        row = lax.broadcasted_iota(jnp.int32, (64, HD), 0)
        column_of = lax.broadcasted_iota(jnp.int32, (64, HD), 1)
        line = jnp.sum(jnp.where(row == column_of, logs, 0.0), axis=0, keepdims=True)
        top = line.astype(BF16).astype(F32)
        middle = (line - top).astype(BF16).astype(F32)
        low = line - top - middle
        which = lax.broadcasted_iota(jnp.int32, (16, HD), 0)
        lines = jnp.where(
            which == 0, top, jnp.where(which == 1, middle, jnp.where(which == 2, low, 0.0))
        )
        out[s, 64:MSG] = lines.astype(BF16)


def finish_kernel(
    ids, table, c0, c1, c2, c3, out_0, lse_0, out_1, lse_1, w0, w1, w2, w3,
    scores, keep, send, held, attention,
):
    for e, ref in enumerate((c0, c1, c2, c3)):
        held[e] = ref[...]
    totals = [[], []]
    for j in range(4):
        message = held[table[40 + j], j]
        lines = message[64:MSG].astype(F32)
        line = (lines[0:1] + lines[1:2]) + lines[2:3]
        logs = column(line, 64)
        for h in range(2):
            rows = slice(j * PER, (j + 1) * PER)
            near_rows = slice((j % 2) * PER, (j % 2 + 1) * PER)
            tail_out, tail_lse = ((out_0, lse_0), (out_1, lse_1))[j // 2]
            prefix_out = message[h * PER : (h + 1) * PER].astype(F32)
            prefix_lse = logs[h * PER : (h + 1) * PER]
            own_lse = tail_lse[h, near_rows][:, 0:1]
            high = jnp.maximum(prefix_lse, own_lse)
            share_a = jnp.exp(prefix_lse - high)
            share_b = jnp.exp(own_lse - high)
            both = share_a + share_b
            merged = (share_a * prefix_out + share_b * tail_out[h, near_rows]) / both
            attention[rows, h * HD : (h + 1) * HD] = merged.astype(BF16)
            totals[h].append(jnp.broadcast_to(high + jnp.log(both), (PER, HD)))
    diagonal = lax.broadcasted_iota(jnp.int32, (ROWS, HD), 0) == lax.broadcasted_iota(
        jnp.int32, (ROWS, HD), 1
    )
    for h in range(2):
        total = jnp.concatenate(totals[h], axis=0)
        scores[h : h + 1] = jnp.sum(jnp.where(diagonal, total, 0.0), axis=0, keepdims=True)
    a, b, core, x = ids[0], ids[1], ids[2], ids[3]
    left = attention[...]
    for e, ref in enumerate((w0, w1, w2, w3)):
        for d in (0, 2):
            right = jnp.concatenate(
                [
                    jnp.concatenate([ref[i, :, h * HD : (h + 1) * HD] for i in (d, d + 1)], axis=1)
                    for h in (2, 3)
                ],
                axis=0,
            )
            both = jnp.dot(left, right, preferred_element_type=F32)
            for i in range(2):
                product = both[:, i * HD : (i + 1) * HD]
                at_a, at_b = lax.rem(a - d - i + 4, 4), lax.rem(b - e + 4, 4)
                block = jnp.where(core == 0, 4 * at_b + at_a, 4 * at_a + at_b)
                mine = (block // 8) == core
                pair = lax.rem(block, 8) // 2
                side = lax.rem(block, 2)

                @pl.when(mine)
                def _():
                    keep[lax.rem(pair - x + 4, 4), side] = product

                @pl.when(jnp.logical_not(mine))
                def _():
                    send[pair, side] = product.astype(BF16)


def first_sum_kernel(ids, keep, got, o0, o1, o2, o3):
    x = ids[3]
    for d in range(4):
        total = keep[d] + got[lax.rem(x + d, 4)].astype(F32)
        if d == 0:
            o0[...] = total
        else:
            (o1, o2, o3)[d - 1][...] = total.astype(BF16)


def second_sum_kernel(ids, o0, g1, g2, g3, hidden, out):
    core, x = ids[2], ids[3]
    for side in range(2):
        total = o0[side] + (
            g1[side].astype(F32) + g2[side].astype(F32) + g3[side].astype(F32)
        )
        at = pl.multiple_of((core * 8 + x * 2 + side) * HD, HD)
        out[side] = (hidden[:, pl.ds(at, HD)].astype(F32) + total).astype(BF16)


def gather_kernel(ids, *refs):
    mine, other, out = refs[:4], refs[4:8], refs[8]
    core, x = ids[2], ids[3]
    for d in range(4):
        for side in range(2):
            at = lax.rem(x - d + 4, 4) * 2 + side
            out[:, pl.ds(pl.multiple_of((core * 8 + at) * HD, HD), HD)] = mine[d][side]
            out[:, pl.ds(pl.multiple_of(((1 - core) * 8 + at) * HD, HD), HD)] = other[d][side]


def split(wide, core):
    z, y = wide // 4, wide % 4
    return jnp.where(core == 0, y, z), jnp.where(core == 0, z, y)


def gather_ring(value, first):
    return [value] + [shift(value, first, step) for step in (1, 2, 3)]


def choose(held, table, base, rows):
    shape = struct((4, rows, HD), BF16)
    sends = call(
        functools.partial(route_kernel, base),
        [shape] * 4,
        [table] + held,
        smem=(0,),
        scratch=[pltpu.VMEM((16, rows, HD), BF16)],
    )
    return [sends[0]] + [shift(sends[step], False, step) for step in (1, 2, 3)]


def body(
    hidden_in, attn_gain, w_qkv, q_gain, k_gain, w_out,
    prefix_cache, tail_cache, prompt_lens, tail_lens, slot_prompt,
):
    wide = lax.axis_index("wide").astype(jnp.int32)
    narrow = lax.axis_index("narrow").astype(jnp.int32)
    core, x = narrow % 2, narrow // 2
    a, b = split(wide, core)
    ids = jnp.stack([a, b, core, x]).astype(jnp.int32)

    channel = jnp.arange(HD, dtype=jnp.int32)
    inverse_freq = jnp.exp((channel % 64).astype(F32) * (-2.0 / HD) * math.log(1000000.0))
    table, angles = call(
        tables_kernel,
        [struct((64,), jnp.int32), struct((ROWS, HD), F32)],
        [ids, slot_prompt, prompt_lens, tail_lens, inverse_freq.reshape(1, HD)],
        smem=(0, 1, 2, 3),
        smem_out=(0,),
        scratch=[pltpu.SMEM((64,), jnp.int32)],
    )
    cosine = jnp.cos(angles)
    sine = jnp.sin(angles) * jnp.where(channel < HD // 2, -1.0, 1.0)[None, :]
    q_gain, k_gain = q_gain.reshape(1, HD), k_gain.reshape(1, HD)

    mixed = jnp.concatenate([w_qkv, w_out[:HD], w_out[HD:]], axis=1)
    near = gather_ring(mixed, True)
    normed = call(
        norm_kernel,
        struct((16, ROWS, HD), BF16),
        [hidden_in, attn_gain.reshape(1, -1)],
        cost=(HINT, 1 << 20),
    )
    near, normed, table = lax.optimization_barrier((near, normed, table))
    near_query, near_other = call(
        pack_kernel, [struct((4, ROWS, 2 * HD), BF16), struct((4, ROWS, 4 * HD), BF16)], near
    )
    far_query = gather_ring(near_query, False)
    far_other = gather_ring(near_other, False)
    queries = call(
        query_kernel,
        struct((4, 64, HD), BF16),
        [ids, normed] + far_query + [q_gain, cosine, sine],
        smem=(0,),
        cost=(2 * ROWS * 256 * 2048, 2 << 20),
    )

    held = gather_ring(queries, True)
    asked = choose(held, table, 0, 64)
    new_cache = call(
        pair_kernel,
        struct((2, ROWS, HD), BF16),
        [ids, normed] + far_other + [k_gain, cosine, sine],
        smem=(0,),
        cost=(2 * ROWS * 256 * 2048, 2 << 20),
    )
    tails = []
    for start in (0, 4):
        tails.append(
            call(
                functools.partial(tail_kernel, start),
                [struct((2, 64, HD), F32), struct((2, 64, HD), F32)],
                [tail_lens, queries, new_cache, tail_cache],
                smem=(0,),
                cost=(2 * 64 * 32 * TLEN * HD, 4 << 20),
            )
        )
    asked, tails[0] = lax.optimization_barrier((asked, tails[0]))
    results = call(
        prefix_kernel,
        struct((4, MSG, HD), BF16),
        [table] + asked + [prefix_cache],
        smem=(0,),
        scratch=[pltpu.VMEM((4, 4, 64, HD), BF16), pltpu.VMEM((PLEN // KB, 64, KB), F32)],
        cost=(2 * 2 * 4 * 64 * PLEN * HD, 8 << 20),
    )
    held = gather_ring(results, True)
    held, tails[1] = lax.optimization_barrier((held, tails[1]))
    homes = choose(held, table, 24, MSG)

    scores, keep, send = call(
        finish_kernel,
        [
            struct((2, ROWS), F32),
            struct((4, 2, ROWS, HD), F32),
            struct((4, 2, ROWS, HD), BF16),
        ],
        [ids, table] + homes + [*tails[0], *tails[1]] + far_other,
        smem=(0, 1),
        scratch=[pltpu.VMEM((4, 4, MSG, HD), BF16), pltpu.VMEM((ROWS, 2 * HD), BF16)],
        cost=(2 * ROWS * 256 * 2048, 3 << 20),
    )
    got = swap_core(send)
    block = struct((2, ROWS, HD), BF16)
    sums = call(
        first_sum_kernel,
        [struct((2, ROWS, HD), F32), block, block, block],
        [ids, keep, got],
        smem=(0,),
    )
    moved = [shift_x(sums[step], step) for step in (1, 2, 3)]
    mine = call(second_sum_kernel, block, [ids, sums[0]] + moved + [hidden_in], smem=(0,))
    ours = [mine] + [shift_x(mine, step) for step in (1, 2, 3)]
    theirs = [swap_core(piece) for piece in ours]
    hidden_out = call(gather_kernel, struct((ROWS, 2048), BF16), [ids] + ours + theirs, smem=(0,))
    return (hidden_out, scores.T, new_cache)


def solution(mesh):
    in_specs = (
        P("wide", None),
        P(),
        P("wide", "narrow"),
        P(),
        P(),
        P("narrow", "wide"),
        P(None, "wide", None, "narrow"),
        P(None, "wide", None, "narrow"),
        P(),
        P("wide"),
        P(),
    )
    out_specs = (P("wide", None), P("wide", "narrow"), P(None, "wide", "narrow"))
    return jax.shard_map(body, mesh=mesh, in_specs=in_specs, out_specs=out_specs, check_vma=False)
```

```python
import functools
import math

import jax
import jax.numpy as jnp
from jax import lax
from jax.experimental import pallas as pl
from jax.experimental.pallas import tpu as pltpu
from jax.sharding import PartitionSpec as P

HD = 128
ROWS = 128
PER = 32
PLEN = 4096
TLEN = 256
KB = 1024
MSG = 80
EPS = 1e-06
NEG = -1e30
CONTRACT = (((1,), (1,)), ((), ()))
HINT = 1 << 34
SCALE = HD ** (-0.5)
LOG2E = 1.4426950408889634
F32 = jnp.float32
BF16 = jnp.bfloat16
AXES = ("wide", "narrow")
SMEM = pltpu.SMEM


def device(z, y, x, core):
    return ((z % 4) * 4 + y % 4) * 8 + (x % 4) * 2 + core


def ring(first, step):
    pairs = []
    for z in range(4):
        for y in range(4):
            for x in range(4):
                for core in range(2):
                    along_y = (core == 0) == first
                    target = device(z, y + step, x, core) if along_y else device(z + step, y, x, core)
                    pairs.append((device(z, y, x, core), target))
    return pairs


def shift(value, first, step):
    return lax.ppermute(value, AXES, ring(first, step))


def shift_pair(value, across):
    pairs = []
    for z in range(4):
        for y in range(4):
            for x in range(4):
                for core in range(2):
                    b = y if core else z
                    to = 3 - b if across else b ^ 1
                    target = device(z, to, x, core) if core else device(to, y, x, core)
                    pairs.append((device(z, y, x, core), target))
    return lax.ppermute(value, AXES, pairs)


def shift_x(value, step):
    return lax.ppermute(value, "narrow", [(n, (n + 2 * step) % 8) for n in range(8)])


def swap_core(value):
    return lax.ppermute(value, "narrow", [(n, n ^ 1) for n in range(8)])


def call(kernel, out_shape, args, smem=(), smem_out=(), hbm=(), hbm_out=False, scratch=(), cost=None):
    def spec(is_scalar, is_far):
        space = SMEM if is_scalar else pltpu.HBM if is_far else pltpu.VMEM
        return pl.BlockSpec(memory_space=space)

    specs = [spec(i in smem, i in hbm) for i in range(len(args))]
    if isinstance(out_shape, (tuple, list)):
        outs = [spec(i in smem_out, False) for i in range(len(out_shape))]
    else:
        outs = spec(False, hbm_out)
    flops, nbytes = cost or (1 << 20, 1 << 20)
    return pl.pallas_call(
        kernel,
        out_shape=out_shape,
        in_specs=specs,
        out_specs=outs,
        scratch_shapes=list(scratch),
        compiler_params=pltpu.CompilerParams(vmem_limit_bytes=8 << 20),
        cost_estimate=pl.CostEstimate(flops=flops, bytes_accessed=nbytes, transcendentals=0),
    )(*args)


def struct(shape, dtype):
    return jax.ShapeDtypeStruct(shape, dtype)


def tables_kernel(ids, prompts, lens, tails, freq, table, angles, inverse):
    a, b, core = ids[0], ids[1], ids[2]
    wide = jnp.where(core == 0, 4 * b + a, 4 * a + b)

    def invert(i, carry):
        inverse[prompts[i]] = i
        return carry

    lax.fori_loop(0, 64, invert, 0, unroll=True)
    for base, source in ((0, prompts), (24, inverse)):
        for e in range(4):
            at_b = lax.rem(b + e, 4)
            there = jnp.where(core == 0, 4 * at_b + a, 4 * a + at_b)
            for k in range(4):
                item = source[there * 4 + k]
                z, y = item // 16, lax.rem(item // 4, 4)
                from_a, from_b = jnp.where(core == 0, y, z), jnp.where(core == 0, z, y)
                table[base + 4 * e + k] = lax.rem(a - from_a + 4, 4) * 4 + lax.rem(item, 4)
                if e == 0:
                    table[base + 16 + k] = lax.rem(b - from_b + 4, 4)
                    table[base + 20 + k] = lens[item]
    row = lax.broadcasted_iota(jnp.int32, (ROWS, HD), 0)
    pair = row // 2
    position = jnp.zeros((ROWS, HD), jnp.int32)
    for c in range(64):
        position = jnp.where(pair == c, lens[wide * 4 + c // 16] + tails[c], position)
    position = position + lax.rem(row, 2)
    angles[...] = position.astype(F32) * freq[...]


def norm_kernel(hidden, gain, out):
    values = hidden[...].astype(F32)
    mean_square = jnp.mean(values * values, axis=-1, keepdims=True)
    factor = lax.rsqrt(mean_square + EPS)
    for block in range(16):
        part = hidden[:, block * HD : (block + 1) * HD].astype(F32) * factor
        out[block] = (part * gain[:, block * HD : (block + 1) * HD]).astype(BF16)


def mix_kernel(w_qkv, w_out, out, sems):
    copies = [
        pltpu.make_async_copy(w_qkv, out.at[:, : 4 * HD], sems.at[0]),
        pltpu.make_async_copy(w_out.at[:HD], out.at[:, 4 * HD : 5 * HD], sems.at[1]),
        pltpu.make_async_copy(w_out.at[HD:], out.at[:, 5 * HD :], sems.at[2]),
    ]
    for copy in copies:
        copy.start()
    for copy in copies:
        copy.wait()


def pack_kernel(w0, w1, w2, w3, first, second):
    for d, ref in enumerate((w0, w1, w2, w3)):
        first[d] = ref[:, : 2 * HD]
        second[d] = ref[:, 2 * HD :]


def around(b, pairs):
    if pairs:
        return [b, b + 1 - 2 * lax.rem(b, 2), 3 - b, 2 - b + 2 * lax.rem(b, 2)]
    return [lax.rem(b - e + 4, 4) for e in range(4)]


def project(ids, normed, refs, pairs):
    a, b, core = ids[0], ids[1], ids[2]
    total = jnp.zeros((ROWS, 2 * HD), F32)
    for e, at_b in enumerate(around(b, pairs)):
        left = []
        for d in range(4):
            at_a = lax.rem(a - d + 4, 4)
            left.append(normed[jnp.where(core == 0, 4 * at_b + at_a, 4 * at_a + at_b)])
        right = jnp.concatenate([refs[e][d, :, : 2 * HD] for d in range(4)], axis=0)
        total = total + jnp.dot(
            jnp.concatenate(left, axis=1), right, preferred_element_type=F32
        )
    return total


def head_norm(values, gain, cosine, sine):
    mean_square = jnp.mean(values * values, axis=-1, keepdims=True)
    values = values * lax.rsqrt(mean_square + EPS) * gain
    return values * cosine + pltpu.roll(values, HD // 2, 1) * sine


def query_kernel(ids, normed, w0, w1, w2, w3, gain, cosine, sine, out):
    total = project(ids, normed, (w0, w1, w2, w3), False)
    for h in range(2):
        head = head_norm(total[:, h * HD : (h + 1) * HD], gain[...], cosine[...], sine[...])
        head = head.astype(BF16)
        for j in range(4):
            out[j, h * PER : (h + 1) * PER] = head[j * PER : (j + 1) * PER]


def own_kernel(
    ids, normed, w0, w1, w2, w3, gain, cosine, sine, queries, acc_0, high_0, acc_1, high_1,
    new_cache, out, lse,
):
    total = project(ids, normed, (w0, w1, w2, w3), True)
    keys = head_norm(total[:, :HD], gain[...], cosine[...], sine[...]).astype(BF16)
    values = total[:, HD:].astype(BF16)
    new_cache[0] = keys
    new_cache[1] = values
    i = lax.broadcasted_iota(jnp.int32, (2 * HD, ROWS), 0)
    key = lax.broadcasted_iota(jnp.int32, (2 * HD, ROWS), 1)
    row = i // 64 * PER + lax.rem(i, PER)
    visible = (row // 2 == key // 2) & (key <= row)
    score = lax.dot_general(
        queries[...].reshape(2 * HD, HD), keys, CONTRACT, preferred_element_type=F32
    )
    score = jnp.where(visible, score, NEG)
    acc = jnp.concatenate([acc_0[...], acc_1[...]], axis=0)
    stats = jnp.concatenate([high_0[...], high_1[...]], axis=0)
    before, sums = stats[:, 0:1], stats[:, 64:65]
    high = jnp.maximum(before, jnp.max(score, axis=1, keepdims=True))
    scale = jnp.exp2((before - high) * (SCALE * LOG2E))
    weight = jnp.exp2((score - high) * (SCALE * LOG2E))
    sums = sums * scale + jnp.sum(weight, axis=1, keepdims=True)
    acc = acc * scale + jnp.dot(weight.astype(BF16), values, preferred_element_type=F32)
    out[...] = acc / sums
    lse[...] = jnp.broadcast_to(high * SCALE + jnp.log(sums), (2 * HD, HD))


def route_kernel(base, index, x0, x1, x2, x3, o0, o1, o2, o3, held):
    for d, ref in enumerate((x0, x1, x2, x3)):
        held[4 * d : 4 * d + 4] = ref[...]
    for e, ref in enumerate((o0, o1, o2, o3)):
        for k in range(4):
            ref[k] = held[index[base + 4 * e + k]]


def column(rows, count):
    lane = lax.broadcasted_iota(jnp.int32, (count, HD), 1)
    row = lax.broadcasted_iota(jnp.int32, (count, HD), 0)
    spread = jnp.broadcast_to(rows, (count, HD))
    return jnp.sum(jnp.where(lane == row, spread, 0.0), axis=1, keepdims=True)


def tail_kernel(start, lens, queries, cache, out, stats):
    conts = 8
    row = lax.broadcasted_iota(jnp.int32, (32, TLEN), 0)
    lane = lax.broadcasted_iota(jnp.int32, (32, TLEN), 1)
    owner = lax.rem(row, 16) // 2
    owner_out = owner[:, :HD]
    for g in range(start, start + 4):
        j, half = g // 2, (g % 2) * 16
        q = jnp.concatenate(
            [queries[j, half : half + 16], queries[j, PER + half : PER + half + 16]], axis=0
        )
        score = jnp.zeros((32, TLEN), F32)
        length = jnp.zeros((32, TLEN), jnp.int32)
        for i in range(conts):
            part = lax.dot_general(
                q, cache[0, g * conts + i], CONTRACT, preferred_element_type=F32
            )
            score = jnp.where(owner == i, part, score)
            length = jnp.where(owner == i, lens[g * conts + i], length)
        score = jnp.where(lane < length, score, NEG)
        high = jnp.max(score, axis=1, keepdims=True)
        weight = jnp.exp2((score - high) * (SCALE * LOG2E))
        sums = jnp.sum(weight, axis=1, keepdims=True)
        weight = weight.astype(BF16)
        acc = jnp.zeros((32, HD), F32)
        for i in range(conts):
            part = jnp.dot(weight, cache[1, g * conts + i], preferred_element_type=F32)
            acc = jnp.where(owner_out == i, part, acc)
        both = jnp.where(lane[:, :HD] < 64, high, sums)
        for h in range(2):
            at = (g - start) // 2 * 64 + h * PER + half
            out[at : at + 16] = acc[h * 16 : h * 16 + 16]
            stats[at : at + 16] = both[h * 16 : h * 16 + 16]


def prefix_kernel(table, r0, r1, r2, r3, cache, out, held, scores):
    select = [table[16 + s] for s in range(4)]
    lens = [table[20 + s] for s in range(4)]
    counts = [(lens[s] + (KB - 1)) // KB for s in range(4)]
    for e, ref in enumerate((r0, r1, r2, r3)):
        held[e] = ref[...]
    lane = lax.broadcasted_iota(jnp.int32, (64, KB), 1)
    for s in range(4):
        q = held[select[s], s]

        def first(i, high):
            block = cache[0, s, pl.ds(pl.multiple_of(i * KB, KB), KB)]
            part = lax.dot_general(q, block, CONTRACT, preferred_element_type=F32)
            part = jnp.where(lane < lens[s] - i * KB, part, NEG)
            scores[i] = part
            for c in range(KB // HD):
                high = jnp.maximum(high, part[:, c * HD : (c + 1) * HD])
            return high

        high = lax.fori_loop(0, counts[s], first, jnp.full((64, HD), NEG, F32))
        high = jnp.max(high, axis=1, keepdims=True)

        def second(i, carry):
            sums, acc = carry
            weight = jnp.exp2((scores[i] - high) * (SCALE * LOG2E))
            for c in range(KB // HD):
                sums = sums + weight[:, c * HD : (c + 1) * HD]
            block = cache[1, s, pl.ds(pl.multiple_of(i * KB, KB), KB)]
            acc = acc + jnp.dot(weight.astype(BF16), block, preferred_element_type=F32)
            return sums, acc

        zero = jnp.zeros((64, HD), F32)
        sums, acc = lax.fori_loop(0, counts[s], second, (zero, zero))
        sums = jnp.sum(sums, axis=1, keepdims=True)
        out[s, :64] = (acc / sums).astype(BF16)
        logs = jnp.broadcast_to(high * SCALE + jnp.log(sums), (64, HD))
        row = lax.broadcasted_iota(jnp.int32, (64, HD), 0)
        column_of = lax.broadcasted_iota(jnp.int32, (64, HD), 1)
        line = jnp.sum(jnp.where(row == column_of, logs, 0.0), axis=0, keepdims=True)
        top = line.astype(BF16).astype(F32)
        middle = (line - top).astype(BF16).astype(F32)
        low = line - top - middle
        which = lax.broadcasted_iota(jnp.int32, (16, HD), 0)
        lines = jnp.where(
            which == 0, top, jnp.where(which == 1, middle, jnp.where(which == 2, low, 0.0))
        )
        out[s, 64:MSG] = lines.astype(BF16)


def finish_kernel(
    ids, table, c0, c1, c2, c3, tail_out, tail_lse, w0, w1, w2, w3,
    scores, keep, send, held, attention, products,
):
    for e, ref in enumerate((c0, c1, c2, c3)):
        held[e] = ref[...]
    totals = [[], []]
    for j in range(4):
        message = held[table[40 + j], j]
        lines = message[64:MSG].astype(F32)
        line = (lines[0:1] + lines[1:2]) + lines[2:3]
        logs = column(line, 64)
        for h in range(2):
            rows = slice(j * PER, (j + 1) * PER)
            own = slice(j * 64 + h * PER, j * 64 + (h + 1) * PER)
            prefix_out = message[h * PER : (h + 1) * PER].astype(F32)
            prefix_lse = logs[h * PER : (h + 1) * PER]
            own_lse = tail_lse[own][:, 0:1]
            high = jnp.maximum(prefix_lse, own_lse)
            share_a = jnp.exp(prefix_lse - high)
            share_b = jnp.exp(own_lse - high)
            both = share_a + share_b
            merged = (share_a * prefix_out + share_b * tail_out[own]) / both
            attention[rows, h * HD : (h + 1) * HD] = merged.astype(BF16)
            totals[h].append(jnp.broadcast_to(high + jnp.log(both), (PER, HD)))
    diagonal = lax.broadcasted_iota(jnp.int32, (ROWS, HD), 0) == lax.broadcasted_iota(
        jnp.int32, (ROWS, HD), 1
    )
    for h in range(2):
        total = jnp.concatenate(totals[h], axis=0)
        scores[h : h + 1] = jnp.sum(jnp.where(diagonal, total, 0.0), axis=0, keepdims=True)
    a, b, core, x = ids[0], ids[1], ids[2], ids[3]
    left = attention[...]
    for ref, at_b in zip((w0, w1, w2, w3), around(b, True)):
        for d in (0, 2):
            right = jnp.concatenate(
                [
                    jnp.concatenate([ref[i, :, h * HD : (h + 1) * HD] for i in (d, d + 1)], axis=1)
                    for h in (2, 3)
                ],
                axis=0,
            )
            both = jnp.dot(left, right, preferred_element_type=F32)
            for i in range(2):
                at_a = lax.rem(a - d - i + 4, 4)
                block = jnp.where(core == 0, 4 * at_b + at_a, 4 * at_a + at_b)
                products[block] = both[:, i * HD : (i + 1) * HD]
    for pair in range(4):
        for side in range(2):
            keep[lax.rem(pair - x + 4, 4), side] = products[core * 8 + pair * 2 + side]
            send[pair, side] = products[(1 - core) * 8 + pair * 2 + side].astype(BF16)


def first_sum_kernel(ids, keep, got, o0, o1, o2, o3):
    x = ids[3]
    for d in range(4):
        total = keep[d] + got[lax.rem(x + d, 4)].astype(F32)
        if d == 0:
            o0[...] = total
        else:
            (o1, o2, o3)[d - 1][...] = total.astype(BF16)


def second_sum_kernel(ids, o0, g1, g2, g3, hidden, out):
    core, x = ids[2], ids[3]
    for side in range(2):
        total = o0[side] + (
            g1[side].astype(F32) + g2[side].astype(F32) + g3[side].astype(F32)
        )
        at = pl.multiple_of((core * 8 + x * 2 + side) * HD, HD)
        out[side] = (hidden[:, pl.ds(at, HD)].astype(F32) + total).astype(BF16)


def gather_kernel(ids, *refs):
    mine, other, out, sems = refs[:4], refs[4:8], refs[8], refs[9]
    core, x = ids[2], ids[3]
    copies = []
    for d in range(4):
        for side in range(2):
            at = lax.rem(x - d + 4, 4) * 2 + side
            for pieces, half in ((mine, core), (other, 1 - core)):
                columns = pl.ds(pl.multiple_of((half * 8 + at) * HD, HD), HD)
                copies.append(
                    pltpu.make_async_copy(
                        pieces[d].at[side], out.at[:, columns], sems.at[len(copies)]
                    )
                )
                copies[-1].start()
    for copy in copies:
        copy.wait()


def split(wide, core):
    z, y = wide // 4, wide % 4
    return jnp.where(core == 0, y, z), jnp.where(core == 0, z, y)


def gather_ring(value, first):
    return [value] + [shift(value, first, step) for step in (1, 2, 3)]


def choose(held, table, base, rows):
    shape = struct((4, rows, HD), BF16)
    sends = call(
        functools.partial(route_kernel, base),
        [shape] * 4,
        [table] + held,
        smem=(0,),
        scratch=[pltpu.VMEM((16, rows, HD), BF16)],
    )
    return [sends[0]] + [shift(sends[step], False, step) for step in (1, 2, 3)]


def body(
    hidden_in, attn_gain, w_qkv, q_gain, k_gain, w_out,
    prefix_cache, tail_cache, prompt_lens, tail_lens, slot_prompt,
):
    wide = lax.axis_index("wide").astype(jnp.int32)
    narrow = lax.axis_index("narrow").astype(jnp.int32)
    core, x = narrow % 2, narrow // 2
    a, b = split(wide, core)
    ids = jnp.stack([a, b, core, x]).astype(jnp.int32)

    channel = jnp.arange(HD, dtype=jnp.int32)
    inverse_freq = jnp.exp((channel % 64).astype(F32) * (-2.0 / HD) * math.log(1000000.0))
    table, angles = call(
        tables_kernel,
        [struct((64,), jnp.int32), struct((ROWS, HD), F32)],
        [ids, slot_prompt, prompt_lens, tail_lens, inverse_freq.reshape(1, HD)],
        smem=(0, 1, 2, 3),
        smem_out=(0,),
        scratch=[pltpu.SMEM((64,), jnp.int32)],
    )
    cosine = jnp.cos(angles)
    sine = jnp.sin(angles) * jnp.where(channel < HD // 2, -1.0, 1.0)[None, :]
    q_gain, k_gain = q_gain.reshape(1, HD), k_gain.reshape(1, HD)

    mixed = call(
        mix_kernel,
        struct((ROWS, 6 * HD), BF16),
        [w_qkv, w_out],
        hbm=(0, 1),
        scratch=[pltpu.SemaphoreType.DMA((3,))],
    )
    near = gather_ring(mixed, True)
    normed = call(
        norm_kernel,
        struct((16, ROWS, HD), BF16),
        [hidden_in, attn_gain.reshape(1, -1)],
        cost=(HINT, 1 << 20),
    )
    near, normed, table = lax.optimization_barrier((near, normed, table))
    near_query, near_other = call(
        pack_kernel, [struct((4, ROWS, 2 * HD), BF16), struct((4, ROWS, 4 * HD), BF16)], near
    )
    far_query = gather_ring(near_query, False)
    beside = shift_pair(near_other, False)
    far_other = [near_other, beside, shift_pair(near_other, True), shift_pair(beside, True)]
    queries = call(
        query_kernel,
        struct((4, 64, HD), BF16),
        [ids, normed] + far_query + [q_gain, cosine, sine],
        smem=(0,),
        cost=(2 * ROWS * 256 * 2048, 2 << 20),
    )

    held = gather_ring(queries, True)
    tails = []
    for start in (0, 4):
        tails.append(
            call(
                functools.partial(tail_kernel, start),
                [struct((HD, HD), F32)] * 2,
                [tail_lens, queries, tail_cache],
                smem=(0,),
                cost=(2 * 64 * 32 * TLEN * HD, 4 << 20),
            )
        )
    held, tails[0] = lax.optimization_barrier((held, tails[0]))
    asked = choose(held, table, 0, 64)
    asked, tails[1] = lax.optimization_barrier((asked, tails[1]))
    results = call(
        prefix_kernel,
        struct((4, MSG, HD), BF16),
        [table] + asked + [prefix_cache],
        smem=(0,),
        scratch=[pltpu.VMEM((4, 4, 64, HD), BF16), pltpu.VMEM((PLEN // KB, 64, KB), F32)],
        cost=(2 * 2 * 4 * 64 * PLEN * HD, 8 << 20),
    )
    held = gather_ring(results, True)
    new_cache, tail_out, tail_lse = call(
        own_kernel,
        [struct((2, ROWS, HD), BF16)] + [struct((2 * HD, HD), F32)] * 2,
        [ids, normed] + far_other + [k_gain, cosine, sine, queries, *tails[0], *tails[1]],
        smem=(0,),
        cost=(2 * ROWS * 256 * 2048, 3 << 20),
    )
    held, tail_out = lax.optimization_barrier((held, tail_out))
    homes = choose(held, table, 24, MSG)

    scores, keep, send = call(
        finish_kernel,
        [
            struct((2, ROWS), F32),
            struct((4, 2, ROWS, HD), F32),
            struct((4, 2, ROWS, HD), BF16),
        ],
        [ids, table] + homes + [tail_out, tail_lse] + far_other,
        smem=(0, 1),
        scratch=[pltpu.VMEM((4, 4, MSG, HD), BF16), pltpu.VMEM((ROWS, 2 * HD), BF16),
            pltpu.VMEM((16, ROWS, HD), F32),
        ],
        cost=(2 * ROWS * 256 * 2048, 3 << 20),
    )
    got = swap_core(send)
    block = struct((2, ROWS, HD), BF16)
    sums = call(
        first_sum_kernel,
        [struct((2, ROWS, HD), F32), block, block, block],
        [ids, keep, got],
        smem=(0,),
    )
    moved = [shift_x(sums[step], step) for step in (1, 2, 3)]
    mine = call(second_sum_kernel, block, [ids, sums[0]] + moved + [hidden_in], smem=(0,))
    ours = [mine] + [shift_x(mine, step) for step in (1, 2, 3)]
    theirs = [swap_core(piece) for piece in ours]
    hidden_out = call(gather_kernel, struct((ROWS, 2048), BF16), [ids] + ours + theirs, smem=(0,), hbm_out=True,
        scratch=[pltpu.SemaphoreType.DMA((16,))],
    )
    return (hidden_out, scores.T, new_cache)


def solution(mesh):
    in_specs = (
        P("wide", None),
        P(),
        P("wide", "narrow"),
        P(),
        P(),
        P("narrow", "wide"),
        P(None, "wide", None, "narrow"),
        P(None, "wide", None, "narrow"),
        P(),
        P("wide"),
        P(),
    )
    out_specs = (P("wide", None), P("wide", "narrow"), P(None, "wide", "narrow"))
    return jax.shard_map(body, mesh=mesh, in_specs=in_specs, out_specs=out_specs, check_vma=False)
```

```python
import functools
import math

import jax
import jax.numpy as jnp
from jax import lax
from jax.experimental import pallas as pl
from jax.experimental.pallas import tpu as pltpu
from jax.sharding import PartitionSpec as P

HD = 128
ROWS = 128
PER = 32
PLEN = 4096
TLEN = 256
FIRST = 2048
LATER = ((2048, 2048),)
MSG = 80
EPS = 1e-06
NEG = -1e30
CONTRACT = (((1,), (1,)), ((), ()))
HINT = 1 << 34
SCALE = HD ** (-0.5)
LOG2E = 1.4426950408889634
F32 = jnp.float32
BF16 = jnp.bfloat16
AXES = ("wide", "narrow")
SMEM = pltpu.SMEM


def device(z, y, x, core):
    return ((z % 4) * 4 + y % 4) * 8 + (x % 4) * 2 + core


def ring(first, step):
    pairs = []
    for z in range(4):
        for y in range(4):
            for x in range(4):
                for core in range(2):
                    along_y = (core == 0) == first
                    target = device(z, y + step, x, core) if along_y else device(z + step, y, x, core)
                    pairs.append((device(z, y, x, core), target))
    return pairs


def shift(value, first, step):
    return lax.ppermute(value, AXES, ring(first, step))


def shift_pair(value, across):
    pairs = []
    for z in range(4):
        for y in range(4):
            for x in range(4):
                for core in range(2):
                    b = y if core else z
                    to = 3 - b if across else b ^ 1
                    target = device(z, to, x, core) if core else device(to, y, x, core)
                    pairs.append((device(z, y, x, core), target))
    return lax.ppermute(value, AXES, pairs)


def shift_x(value, step):
    return lax.ppermute(value, "narrow", [(n, (n + 2 * step) % 8) for n in range(8)])


def swap_core(value):
    return lax.ppermute(value, "narrow", [(n, n ^ 1) for n in range(8)])


def call(
    kernel, out_shape, args, smem=(), smem_out=(), hbm=(), hbm_out=False, scratch=(), cost=None,
    grant=8 << 20,
):
    def spec(is_scalar, is_far):
        space = SMEM if is_scalar else pltpu.HBM if is_far else pltpu.VMEM
        return pl.BlockSpec(memory_space=space)

    specs = [spec(i in smem, i in hbm) for i in range(len(args))]
    if isinstance(out_shape, (tuple, list)):
        outs = [spec(i in smem_out, False) for i in range(len(out_shape))]
    else:
        outs = spec(False, hbm_out)
    flops, nbytes = cost or (1 << 20, 1 << 20)
    return pl.pallas_call(
        kernel,
        out_shape=out_shape,
        in_specs=specs,
        out_specs=outs,
        scratch_shapes=list(scratch),
        compiler_params=pltpu.CompilerParams(vmem_limit_bytes=grant),
        cost_estimate=pl.CostEstimate(flops=flops, bytes_accessed=nbytes, transcendentals=0),
    )(*args)


def struct(shape, dtype):
    return jax.ShapeDtypeStruct(shape, dtype)


def tables_kernel(ids, prompts, lens, tails, freq, table, angles, inverse):
    a, b, core = ids[0], ids[1], ids[2]
    wide = jnp.where(core == 0, 4 * b + a, 4 * a + b)

    def invert(i, carry):
        inverse[prompts[i]] = i
        return carry

    lax.fori_loop(0, 64, invert, 0, unroll=True)
    for base, source in ((0, prompts), (24, inverse)):
        for e in range(4):
            at_b = lax.rem(b + e, 4)
            there = jnp.where(core == 0, 4 * at_b + a, 4 * a + at_b)
            for k in range(4):
                item = source[there * 4 + k]
                z, y = item // 16, lax.rem(item // 4, 4)
                from_a, from_b = jnp.where(core == 0, y, z), jnp.where(core == 0, z, y)
                table[base + 4 * e + k] = lax.rem(a - from_a + 4, 4) * 4 + lax.rem(item, 4)
                if e == 0:
                    table[base + 16 + k] = lax.rem(b - from_b + 4, 4)
                    table[base + 20 + k] = lens[item]
    row = lax.broadcasted_iota(jnp.int32, (ROWS, HD), 0)
    pair = row // 2
    position = jnp.zeros((ROWS, HD), jnp.int32)
    for c in range(64):
        position = jnp.where(pair == c, lens[wide * 4 + c // 16] + tails[c], position)
    position = position + lax.rem(row, 2)
    angles[...] = position.astype(F32) * freq[...]


def norm_kernel(hidden, gain, out):
    values = hidden[...].astype(F32)
    mean_square = jnp.mean(values * values, axis=-1, keepdims=True)
    factor = lax.rsqrt(mean_square + EPS)
    for block in range(16):
        part = hidden[:, block * HD : (block + 1) * HD].astype(F32) * factor
        out[block] = (part * gain[:, block * HD : (block + 1) * HD]).astype(BF16)


def mix_kernel(w_qkv, w_out, out, sems):
    copies = [
        pltpu.make_async_copy(w_qkv, out.at[:, : 4 * HD], sems.at[0]),
        pltpu.make_async_copy(w_out.at[:HD], out.at[:, 4 * HD : 5 * HD], sems.at[1]),
        pltpu.make_async_copy(w_out.at[HD:], out.at[:, 5 * HD :], sems.at[2]),
    ]
    for copy in copies:
        copy.start()
    for copy in copies:
        copy.wait()


def pack_kernel(w0, w1, w2, w3, first, second):
    for d, ref in enumerate((w0, w1, w2, w3)):
        first[d] = ref[:, : 2 * HD]
        second[d] = ref[:, 2 * HD :]


def around(b, pairs):
    if pairs:
        return [b, b + 1 - 2 * lax.rem(b, 2), 3 - b, 2 - b + 2 * lax.rem(b, 2)]
    return [lax.rem(b - e + 4, 4) for e in range(4)]


def project(ids, normed, refs, pairs):
    a, b, core = ids[0], ids[1], ids[2]
    total = jnp.zeros((ROWS, 2 * HD), F32)
    for e, at_b in enumerate(around(b, pairs)):
        left = []
        for d in range(4):
            at_a = lax.rem(a - d + 4, 4)
            left.append(normed[jnp.where(core == 0, 4 * at_b + at_a, 4 * at_a + at_b)])
        right = jnp.concatenate([refs[e][d, :, : 2 * HD] for d in range(4)], axis=0)
        total = total + jnp.dot(
            jnp.concatenate(left, axis=1), right, preferred_element_type=F32
        )
    return total


def head_norm(values, gain, cosine, sine):
    mean_square = jnp.mean(values * values, axis=-1, keepdims=True)
    values = values * lax.rsqrt(mean_square + EPS) * gain
    return values * cosine + pltpu.roll(values, HD // 2, 1) * sine


def query_kernel(ids, normed, w0, w1, w2, w3, gain, cosine, sine, out):
    total = project(ids, normed, (w0, w1, w2, w3), False)
    for h in range(2):
        head = head_norm(total[:, h * HD : (h + 1) * HD], gain[...], cosine[...], sine[...])
        head = head.astype(BF16)
        for j in range(4):
            out[j, h * PER : (h + 1) * PER] = head[j * PER : (j + 1) * PER]


def own_kernel(
    ids, normed, w0, w1, w2, w3, gain, cosine, sine, queries, acc_0, high_0, acc_1, high_1,
    new_cache, out, lse,
):
    total = project(ids, normed, (w0, w1, w2, w3), True)
    keys = head_norm(total[:, :HD], gain[...], cosine[...], sine[...]).astype(BF16)
    values = total[:, HD:].astype(BF16)
    new_cache[0] = keys
    new_cache[1] = values
    i = lax.broadcasted_iota(jnp.int32, (2 * HD, ROWS), 0)
    key = lax.broadcasted_iota(jnp.int32, (2 * HD, ROWS), 1)
    row = i // 64 * PER + lax.rem(i, PER)
    visible = (row // 2 == key // 2) & (key <= row)
    score = lax.dot_general(
        queries[...].reshape(2 * HD, HD), keys, CONTRACT, preferred_element_type=F32
    )
    score = jnp.where(visible, score, NEG)
    acc = jnp.concatenate([acc_0[...], acc_1[...]], axis=0)
    stats = jnp.concatenate([high_0[...], high_1[...]], axis=0)
    before, sums = stats[:, 0:1], stats[:, 64:65]
    high = jnp.maximum(before, jnp.max(score, axis=1, keepdims=True))
    scale = jnp.exp2((before - high) * (SCALE * LOG2E))
    weight = jnp.exp2((score - high) * (SCALE * LOG2E))
    sums = sums * scale + jnp.sum(weight, axis=1, keepdims=True)
    acc = acc * scale + jnp.dot(weight.astype(BF16), values, preferred_element_type=F32)
    out[...] = acc / sums
    lse[...] = jnp.broadcast_to(high * SCALE + jnp.log(sums), (2 * HD, HD))


def route_kernel(base, index, x0, x1, x2, x3, o0, o1, o2, o3, held):
    for d, ref in enumerate((x0, x1, x2, x3)):
        held[4 * d : 4 * d + 4] = ref[...]
    for e, ref in enumerate((o0, o1, o2, o3)):
        for k in range(4):
            ref[k] = held[index[base + 4 * e + k]]


def column(rows, count):
    lane = lax.broadcasted_iota(jnp.int32, (count, HD), 1)
    row = lax.broadcasted_iota(jnp.int32, (count, HD), 0)
    spread = jnp.broadcast_to(rows, (count, HD))
    return jnp.sum(jnp.where(lane == row, spread, 0.0), axis=1, keepdims=True)


def tail_kernel(start, lens, queries, cache, out, stats):
    conts = 8
    row = lax.broadcasted_iota(jnp.int32, (32, TLEN), 0)
    lane = lax.broadcasted_iota(jnp.int32, (32, TLEN), 1)
    owner = lax.rem(row, 16) // 2
    owner_out = owner[:, :HD]
    for g in range(start, start + 4):
        j, half = g // 2, (g % 2) * 16
        q = jnp.concatenate(
            [queries[j, half : half + 16], queries[j, PER + half : PER + half + 16]], axis=0
        )
        score = jnp.zeros((32, TLEN), F32)
        length = jnp.zeros((32, TLEN), jnp.int32)
        for i in range(conts):
            part = lax.dot_general(
                q, cache[0, g * conts + i], CONTRACT, preferred_element_type=F32
            )
            score = jnp.where(owner == i, part, score)
            length = jnp.where(owner == i, lens[g * conts + i], length)
        score = jnp.where(lane < length, score, NEG)
        high = jnp.max(score, axis=1, keepdims=True)
        weight = jnp.exp2((score - high) * (SCALE * LOG2E))
        sums = jnp.sum(weight, axis=1, keepdims=True)
        weight = weight.astype(BF16)
        acc = jnp.zeros((32, HD), F32)
        for i in range(conts):
            part = jnp.dot(weight, cache[1, g * conts + i], preferred_element_type=F32)
            acc = jnp.where(owner_out == i, part, acc)
        both = jnp.where(lane[:, :HD] < 64, high, sums)
        for h in range(2):
            at = (g - start) // 2 * 64 + h * PER + half
            out[at : at + 16] = acc[h * 16 : h * 16 + 16]
            stats[at : at + 16] = both[h * 16 : h * 16 + 16]


def prefix_kernel(table, r0, r1, r2, r3, cache, out, held, scores, highs, totals, accs):
    lens = [table[20 + s] for s in range(4)]
    for e, ref in enumerate((r0, r1, r2, r3)):
        held[e] = ref[...]
    queries = [held[table[16 + s], s] for s in range(4)]

    def first(s, start, size, high):
        block = cache[0, s, pl.ds(start, size)]
        part = lax.dot_general(queries[s], block, CONTRACT, preferred_element_type=F32)
        lane = lax.broadcasted_iota(jnp.int32, (64, size), 1)
        part = jnp.where(lane < lens[s] - start, part, NEG)
        for c in range(size // HD):
            piece = part[:, c * HD : (c + 1) * HD]
            scores[s, start // HD + c] = piece
            high = piece if high is None else jnp.maximum(high, piece)
        return high

    def second(s, start, size, high, sums, acc):
        weights = []
        for c in range(size // HD):
            weight = jnp.exp2((scores[s, start // HD + c] - high) * (SCALE * LOG2E))
            sums = weight if sums is None else sums + weight
            weights.append(weight.astype(BF16))
        block = cache[1, s, pl.ds(start, size)]
        more = jnp.dot(jnp.concatenate(weights, axis=1), block, preferred_element_type=F32)
        return sums, more if acc is None else acc + more

    for s in range(4):
        highs[s] = first(s, 0, FIRST, None)
    for start, size in LATER:
        for s in range(4):

            @pl.when(lens[s] > start)
            def _():
                highs[s] = first(s, start, size, highs[s])

    for s in range(4):
        highs[s] = jnp.broadcast_to(jnp.max(highs[s], axis=1, keepdims=True), (64, HD))
    for s in range(4):
        totals[s], accs[s] = second(s, 0, FIRST, highs[s], None, None)
    for start, size in LATER:
        for s in range(4):

            @pl.when(lens[s] > start)
            def _():
                totals[s], accs[s] = second(s, start, size, highs[s], totals[s], accs[s])

    row = lax.broadcasted_iota(jnp.int32, (64, HD), 0)
    column_of = lax.broadcasted_iota(jnp.int32, (64, HD), 1)
    which = lax.broadcasted_iota(jnp.int32, (16, HD), 0)
    for s in range(4):
        sums = jnp.broadcast_to(jnp.sum(totals[s], axis=1, keepdims=True), (64, HD))
        out[s, :64] = (accs[s] / sums).astype(BF16)
        logs = highs[s] * SCALE + jnp.log(sums)
        line = jnp.sum(jnp.where(row == column_of, logs, 0.0), axis=0, keepdims=True)
        top = line.astype(BF16).astype(F32)
        middle = (line - top).astype(BF16).astype(F32)
        low = line - top - middle
        lines = jnp.where(
            which == 0, top, jnp.where(which == 1, middle, jnp.where(which == 2, low, 0.0))
        )
        out[s, 64:MSG] = lines.astype(BF16)


def prefix_scratch():
    part = pltpu.VMEM((4, 64, HD), F32)
    return [
        pltpu.VMEM((4, 4, 64, HD), BF16),
        pltpu.VMEM((4, PLEN // HD, 64, HD), F32),
        part,
        part,
        part,
    ]


def finish_kernel(
    ids, table, c0, c1, c2, c3, tail_out, tail_lse, w0, w1, w2, w3,
    scores, keep, send, held, attention, products,
):
    for e, ref in enumerate((c0, c1, c2, c3)):
        held[e] = ref[...]
    totals = [[], []]
    for j in range(4):
        message = held[table[40 + j], j]
        lines = message[64:MSG].astype(F32)
        line = (lines[0:1] + lines[1:2]) + lines[2:3]
        logs = column(line, 64)
        for h in range(2):
            rows = slice(j * PER, (j + 1) * PER)
            own = slice(j * 64 + h * PER, j * 64 + (h + 1) * PER)
            prefix_out = message[h * PER : (h + 1) * PER].astype(F32)
            prefix_lse = logs[h * PER : (h + 1) * PER]
            own_lse = tail_lse[own][:, 0:1]
            high = jnp.maximum(prefix_lse, own_lse)
            share_a = jnp.exp(prefix_lse - high)
            share_b = jnp.exp(own_lse - high)
            both = share_a + share_b
            merged = (share_a * prefix_out + share_b * tail_out[own]) / both
            attention[rows, h * HD : (h + 1) * HD] = merged.astype(BF16)
            totals[h].append(jnp.broadcast_to(high + jnp.log(both), (PER, HD)))
    diagonal = lax.broadcasted_iota(jnp.int32, (ROWS, HD), 0) == lax.broadcasted_iota(
        jnp.int32, (ROWS, HD), 1
    )
    for h in range(2):
        total = jnp.concatenate(totals[h], axis=0)
        scores[h : h + 1] = jnp.sum(jnp.where(diagonal, total, 0.0), axis=0, keepdims=True)
    a, b, core, x = ids[0], ids[1], ids[2], ids[3]
    left = attention[...]
    for ref, at_b in zip((w0, w1, w2, w3), around(b, True)):
        for d in (0, 2):
            right = jnp.concatenate(
                [
                    jnp.concatenate([ref[i, :, h * HD : (h + 1) * HD] for i in (d, d + 1)], axis=1)
                    for h in (2, 3)
                ],
                axis=0,
            )
            both = jnp.dot(left, right, preferred_element_type=F32)
            for i in range(2):
                at_a = lax.rem(a - d - i + 4, 4)
                block = jnp.where(core == 0, 4 * at_b + at_a, 4 * at_a + at_b)
                products[block] = both[:, i * HD : (i + 1) * HD]
    for pair in range(4):
        for side in range(2):
            keep[lax.rem(pair - x + 4, 4), side] = products[core * 8 + pair * 2 + side]
            send[pair, side] = products[(1 - core) * 8 + pair * 2 + side].astype(BF16)


def first_sum_kernel(ids, keep, got, o0, o1, o2, o3):
    x = ids[3]
    for d in range(4):
        total = keep[d] + got[lax.rem(x + d, 4)].astype(F32)
        if d == 0:
            o0[...] = total
        else:
            (o1, o2, o3)[d - 1][...] = total.astype(BF16)


def second_sum_kernel(ids, o0, g1, g2, g3, hidden, out):
    core, x = ids[2], ids[3]
    for side in range(2):
        total = o0[side] + (
            g1[side].astype(F32) + g2[side].astype(F32) + g3[side].astype(F32)
        )
        at = pl.multiple_of((core * 8 + x * 2 + side) * HD, HD)
        out[side] = (hidden[:, pl.ds(at, HD)].astype(F32) + total).astype(BF16)


def gather_kernel(ids, *refs):
    mine, other, out, sems = refs[:4], refs[4:8], refs[8], refs[9]
    core, x = ids[2], ids[3]
    copies = []
    for d in range(4):
        for side in range(2):
            at = lax.rem(x - d + 4, 4) * 2 + side
            for pieces, half in ((mine, core), (other, 1 - core)):
                columns = pl.ds(pl.multiple_of((half * 8 + at) * HD, HD), HD)
                copies.append(
                    pltpu.make_async_copy(
                        pieces[d].at[side], out.at[:, columns], sems.at[len(copies)]
                    )
                )
                copies[-1].start()
    for copy in copies:
        copy.wait()


def split(wide, core):
    z, y = wide // 4, wide % 4
    return jnp.where(core == 0, y, z), jnp.where(core == 0, z, y)


def gather_ring(value, first):
    return [value] + [shift(value, first, step) for step in (1, 2, 3)]


def choose(held, table, base, rows):
    shape = struct((4, rows, HD), BF16)
    sends = call(
        functools.partial(route_kernel, base),
        [shape] * 4,
        [table] + held,
        smem=(0,),
        scratch=[pltpu.VMEM((16, rows, HD), BF16)],
    )
    return [sends[0]] + [shift(sends[step], False, step) for step in (1, 2, 3)]


def body(
    hidden_in, attn_gain, w_qkv, q_gain, k_gain, w_out,
    prefix_cache, tail_cache, prompt_lens, tail_lens, slot_prompt,
):
    wide = lax.axis_index("wide").astype(jnp.int32)
    narrow = lax.axis_index("narrow").astype(jnp.int32)
    core, x = narrow % 2, narrow // 2
    a, b = split(wide, core)
    ids = jnp.stack([a, b, core, x]).astype(jnp.int32)

    channel = jnp.arange(HD, dtype=jnp.int32)
    inverse_freq = jnp.exp((channel % 64).astype(F32) * (-2.0 / HD) * math.log(1000000.0))
    table, angles = call(
        tables_kernel,
        [struct((64,), jnp.int32), struct((ROWS, HD), F32)],
        [ids, slot_prompt, prompt_lens, tail_lens, inverse_freq.reshape(1, HD)],
        smem=(0, 1, 2, 3),
        smem_out=(0,),
        scratch=[pltpu.SMEM((64,), jnp.int32)],
    )
    cosine = jnp.cos(angles)
    sine = jnp.sin(angles) * jnp.where(channel < HD // 2, -1.0, 1.0)[None, :]
    q_gain, k_gain = q_gain.reshape(1, HD), k_gain.reshape(1, HD)

    mixed = call(
        mix_kernel,
        struct((ROWS, 6 * HD), BF16),
        [w_qkv, w_out],
        hbm=(0, 1),
        scratch=[pltpu.SemaphoreType.DMA((3,))],
        grant=60 << 20,
    )
    near = gather_ring(mixed, True)
    normed = call(
        norm_kernel,
        struct((16, ROWS, HD), BF16),
        [hidden_in, attn_gain.reshape(1, -1)],
        cost=(HINT, 1 << 20),
    )
    near, normed, table = lax.optimization_barrier((near, normed, table))
    near_query, near_other = call(
        pack_kernel, [struct((4, ROWS, 2 * HD), BF16), struct((4, ROWS, 4 * HD), BF16)], near
    )
    far_query = gather_ring(near_query, False)
    beside = shift_pair(near_other, False)
    far_other = [near_other, beside, shift_pair(near_other, True), shift_pair(beside, True)]
    queries = call(
        query_kernel,
        struct((4, 64, HD), BF16),
        [ids, normed] + far_query + [q_gain, cosine, sine],
        smem=(0,),
        cost=(2 * ROWS * 256 * 2048, 2 << 20),
    )

    held = gather_ring(queries, True)
    tails = []
    for start in (0, 4):
        tails.append(
            call(
                functools.partial(tail_kernel, start),
                [struct((HD, HD), F32)] * 2,
                [tail_lens, queries, tail_cache],
                smem=(0,),
                cost=(2 * 64 * 32 * TLEN * HD, 4 << 20),
            )
        )
    held, tails[0] = lax.optimization_barrier((held, tails[0]))
    asked = choose(held, table, 0, 64)
    asked, tails[1] = lax.optimization_barrier((asked, tails[1]))
    results = call(
        prefix_kernel,
        struct((4, MSG, HD), BF16),
        [table] + asked + [prefix_cache],
        smem=(0,),
        scratch=prefix_scratch(),
        cost=(2 * 2 * 4 * 64 * PLEN * HD, 8 << 20),
    )
    held = gather_ring(results, True)
    new_cache, tail_out, tail_lse = call(
        own_kernel,
        [struct((2, ROWS, HD), BF16)] + [struct((2 * HD, HD), F32)] * 2,
        [ids, normed] + far_other + [k_gain, cosine, sine, queries, *tails[0], *tails[1]],
        smem=(0,),
        cost=(2 * ROWS * 256 * 2048, 3 << 20),
    )
    held, tail_out = lax.optimization_barrier((held, tail_out))
    homes = choose(held, table, 24, MSG)

    scores, keep, send = call(
        finish_kernel,
        [
            struct((2, ROWS), F32),
            struct((4, 2, ROWS, HD), F32),
            struct((4, 2, ROWS, HD), BF16),
        ],
        [ids, table] + homes + [tail_out, tail_lse] + far_other,
        smem=(0, 1),
        scratch=[pltpu.VMEM((4, 4, MSG, HD), BF16), pltpu.VMEM((ROWS, 2 * HD), BF16),
            pltpu.VMEM((16, ROWS, HD), F32),
        ],
        cost=(2 * ROWS * 256 * 2048, 3 << 20),
    )
    got = swap_core(send)
    block = struct((2, ROWS, HD), BF16)
    sums = call(
        first_sum_kernel,
        [struct((2, ROWS, HD), F32), block, block, block],
        [ids, keep, got],
        smem=(0,),
    )
    moved = [shift_x(sums[step], step) for step in (1, 2, 3)]
    mine = call(second_sum_kernel, block, [ids, sums[0]] + moved + [hidden_in], smem=(0,))
    ours = [mine] + [shift_x(mine, step) for step in (1, 2, 3)]
    theirs = [swap_core(piece) for piece in ours]
    hidden_out = call(gather_kernel, struct((ROWS, 2048), BF16), [ids] + ours + theirs, smem=(0,), hbm_out=True,
        scratch=[pltpu.SemaphoreType.DMA((16,))],
    )
    return (hidden_out, scores.T, new_cache)


def solution(mesh):
    in_specs = (
        P("wide", None),
        P(),
        P("wide", "narrow"),
        P(),
        P(),
        P("narrow", "wide"),
        P(None, "wide", None, "narrow"),
        P(None, "wide", None, "narrow"),
        P(),
        P("wide"),
        P(),
    )
    out_specs = (P("wide", None), P("wide", "narrow"), P(None, "wide", "narrow"))
    return jax.shard_map(body, mesh=mesh, in_specs=in_specs, out_specs=out_specs, check_vma=False)
```

```python
import functools
import math

import jax
import jax.numpy as jnp
from jax import lax
from jax.experimental import pallas as pl
from jax.experimental.pallas import tpu as pltpu
from jax.sharding import PartitionSpec as P

HD = 128
ROWS = 128
PER = 32
PLEN = 4096
TLEN = 256
FIRST = 2048
LATER = ((2048, 1024), (3072, 1024))
MSG = 80
EPS = 1e-06
NEG = -1e30
CONTRACT = (((1,), (1,)), ((), ()))
HINT = 1 << 34
SCALE = HD ** (-0.5)
LOG2E = 1.4426950408889634
F32 = jnp.float32
BF16 = jnp.bfloat16
AXES = ("wide", "narrow")
SMEM = pltpu.SMEM


def device(z, y, x, core):
    return ((z % 4) * 4 + y % 4) * 8 + (x % 4) * 2 + core


def ring(first, step):
    pairs = []
    for z in range(4):
        for y in range(4):
            for x in range(4):
                for core in range(2):
                    along_y = (core == 0) == first
                    target = device(z, y + step, x, core) if along_y else device(z + step, y, x, core)
                    pairs.append((device(z, y, x, core), target))
    return pairs


def shift(value, first, step):
    return lax.ppermute(value, AXES, ring(first, step))


def shift_pair(value, across):
    pairs = []
    for z in range(4):
        for y in range(4):
            for x in range(4):
                for core in range(2):
                    b = y if core else z
                    to = 3 - b if across else b ^ 1
                    target = device(z, to, x, core) if core else device(to, y, x, core)
                    pairs.append((device(z, y, x, core), target))
    return lax.ppermute(value, AXES, pairs)


def shift_x(value, step):
    return lax.ppermute(value, "narrow", [(n, (n + 2 * step) % 8) for n in range(8)])


def swap_core(value):
    return lax.ppermute(value, "narrow", [(n, n ^ 1) for n in range(8)])


def call(
    kernel, out_shape, args, smem=(), smem_out=(), hbm=(), hbm_out=False, scratch=(), cost=None,
    grant=8 << 20,
):
    def spec(is_scalar, is_far):
        space = SMEM if is_scalar else pltpu.HBM if is_far else pltpu.VMEM
        return pl.BlockSpec(memory_space=space)

    specs = [spec(i in smem, i in hbm) for i in range(len(args))]
    if isinstance(out_shape, (tuple, list)):
        outs = [spec(i in smem_out, False) for i in range(len(out_shape))]
    else:
        outs = spec(False, hbm_out)
    flops, nbytes = cost or (1 << 20, 1 << 20)
    return pl.pallas_call(
        kernel,
        out_shape=out_shape,
        in_specs=specs,
        out_specs=outs,
        scratch_shapes=list(scratch),
        compiler_params=pltpu.CompilerParams(vmem_limit_bytes=grant),
        cost_estimate=pl.CostEstimate(flops=flops, bytes_accessed=nbytes, transcendentals=0),
    )(*args)


def struct(shape, dtype):
    return jax.ShapeDtypeStruct(shape, dtype)


def tables_kernel(ids, prompts, lens, tails, freq, table, angles, inverse):
    a, b, core = ids[0], ids[1], ids[2]
    wide = jnp.where(core == 0, 4 * b + a, 4 * a + b)

    def invert(i, carry):
        inverse[prompts[i]] = i
        return carry

    lax.fori_loop(0, 64, invert, 0, unroll=True)
    for base, source in ((0, prompts), (24, inverse)):
        for e in range(4):
            at_b = lax.rem(b + e, 4)
            there = jnp.where(core == 0, 4 * at_b + a, 4 * a + at_b)
            for k in range(4):
                item = source[there * 4 + k]
                z, y = item // 16, lax.rem(item // 4, 4)
                from_a, from_b = jnp.where(core == 0, y, z), jnp.where(core == 0, z, y)
                table[base + 4 * e + k] = lax.rem(a - from_a + 4, 4) * 4 + lax.rem(item, 4)
                if e == 0:
                    table[base + 16 + k] = lax.rem(b - from_b + 4, 4)
                    table[base + 20 + k] = lens[item]
    row = lax.broadcasted_iota(jnp.int32, (ROWS, HD), 0)
    pair = row // 2
    position = jnp.zeros((ROWS, HD), jnp.int32)
    for c in range(64):
        position = jnp.where(pair == c, lens[wide * 4 + c // 16] + tails[c], position)
    position = position + lax.rem(row, 2)
    angles[...] = position.astype(F32) * freq[...]


def norm_kernel(hidden, gain, out):
    values = hidden[...].astype(F32)
    mean_square = jnp.mean(values * values, axis=-1, keepdims=True)
    factor = lax.rsqrt(mean_square + EPS)
    for block in range(16):
        part = hidden[:, block * HD : (block + 1) * HD].astype(F32) * factor
        out[block] = (part * gain[:, block * HD : (block + 1) * HD]).astype(BF16)


def mix_kernel(w_qkv, w_out, out, sems):
    copies = [
        pltpu.make_async_copy(w_qkv, out.at[:, : 4 * HD], sems.at[0]),
        pltpu.make_async_copy(w_out.at[:HD], out.at[:, 4 * HD : 5 * HD], sems.at[1]),
        pltpu.make_async_copy(w_out.at[HD:], out.at[:, 5 * HD :], sems.at[2]),
    ]
    for copy in copies:
        copy.start()
    for copy in copies:
        copy.wait()


def pack_kernel(w0, w1, w2, w3, first, second):
    for d, ref in enumerate((w0, w1, w2, w3)):
        first[d] = ref[:, : 2 * HD]
        second[d] = ref[:, 2 * HD :]


def around(b, pairs):
    if pairs:
        return [b, b + 1 - 2 * lax.rem(b, 2), 3 - b, 2 - b + 2 * lax.rem(b, 2)]
    return [lax.rem(b - e + 4, 4) for e in range(4)]


def project(ids, normed, refs, pairs):
    a, b, core = ids[0], ids[1], ids[2]
    total = jnp.zeros((ROWS, 2 * HD), F32)
    for e, at_b in enumerate(around(b, pairs)):
        left = []
        for d in range(4):
            at_a = lax.rem(a - d + 4, 4)
            left.append(normed[jnp.where(core == 0, 4 * at_b + at_a, 4 * at_a + at_b)])
        right = jnp.concatenate([refs[e][d, :, : 2 * HD] for d in range(4)], axis=0)
        total = total + jnp.dot(
            jnp.concatenate(left, axis=1), right, preferred_element_type=F32
        )
    return total


def head_norm(values, gain, cosine, sine):
    mean_square = jnp.mean(values * values, axis=-1, keepdims=True)
    values = values * lax.rsqrt(mean_square + EPS) * gain
    return values * cosine + pltpu.roll(values, HD // 2, 1) * sine


def query_kernel(ids, normed, w0, w1, w2, w3, gain, cosine, sine, out):
    total = project(ids, normed, (w0, w1, w2, w3), False)
    for h in range(2):
        head = head_norm(total[:, h * HD : (h + 1) * HD], gain[...], cosine[...], sine[...])
        head = head.astype(BF16)
        for j in range(4):
            out[j, h * PER : (h + 1) * PER] = head[j * PER : (j + 1) * PER]


def own_kernel(
    ids, normed, w0, w1, w2, w3, gain, cosine, sine, queries, acc_0, high_0, acc_1, high_1,
    new_cache, out, lse,
):
    total = project(ids, normed, (w0, w1, w2, w3), True)
    keys = head_norm(total[:, :HD], gain[...], cosine[...], sine[...]).astype(BF16)
    values = total[:, HD:].astype(BF16)
    new_cache[0] = keys
    new_cache[1] = values
    i = lax.broadcasted_iota(jnp.int32, (2 * HD, ROWS), 0)
    key = lax.broadcasted_iota(jnp.int32, (2 * HD, ROWS), 1)
    row = i // 64 * PER + lax.rem(i, PER)
    visible = (row // 2 == key // 2) & (key <= row)
    score = lax.dot_general(
        queries[...].reshape(2 * HD, HD), keys, CONTRACT, preferred_element_type=F32
    )
    score = jnp.where(visible, score, NEG)
    acc = jnp.concatenate([acc_0[...], acc_1[...]], axis=0)
    stats = jnp.concatenate([high_0[...], high_1[...]], axis=0)
    before, sums = stats[:, 0:1], stats[:, 64:65]
    high = jnp.maximum(before, jnp.max(score, axis=1, keepdims=True))
    scale = jnp.exp2((before - high) * (SCALE * LOG2E))
    weight = jnp.exp2((score - high) * (SCALE * LOG2E))
    sums = sums * scale + jnp.sum(weight, axis=1, keepdims=True)
    acc = acc * scale + jnp.dot(weight.astype(BF16), values, preferred_element_type=F32)
    out[...] = acc / sums
    lse[...] = jnp.broadcast_to(high * SCALE + jnp.log(sums), (2 * HD, HD))


def route_kernel(base, index, x0, x1, x2, x3, o0, o1, o2, o3, held):
    for d, ref in enumerate((x0, x1, x2, x3)):
        held[4 * d : 4 * d + 4] = ref[...]
    for e, ref in enumerate((o0, o1, o2, o3)):
        for k in range(4):
            ref[k] = held[index[base + 4 * e + k]]


def column(rows, count):
    lane = lax.broadcasted_iota(jnp.int32, (count, HD), 1)
    row = lax.broadcasted_iota(jnp.int32, (count, HD), 0)
    spread = jnp.broadcast_to(rows, (count, HD))
    return jnp.sum(jnp.where(lane == row, spread, 0.0), axis=1, keepdims=True)


def tail_kernel(start, lens, queries, cache, out, stats):
    conts = 8
    row = lax.broadcasted_iota(jnp.int32, (32, TLEN), 0)
    lane = lax.broadcasted_iota(jnp.int32, (32, TLEN), 1)
    owner = lax.rem(row, 16) // 2
    owner_out = owner[:, :HD]
    for g in range(start, start + 4):
        j, half = g // 2, (g % 2) * 16
        q = jnp.concatenate(
            [queries[j, half : half + 16], queries[j, PER + half : PER + half + 16]], axis=0
        )
        score = jnp.zeros((32, TLEN), F32)
        length = jnp.zeros((32, TLEN), jnp.int32)
        for i in range(conts):
            part = lax.dot_general(
                q, cache[0, g * conts + i], CONTRACT, preferred_element_type=F32
            )
            score = jnp.where(owner == i, part, score)
            length = jnp.where(owner == i, lens[g * conts + i], length)
        score = jnp.where(lane < length, score, NEG)
        high = jnp.max(score, axis=1, keepdims=True)
        weight = jnp.exp2((score - high) * (SCALE * LOG2E))
        sums = jnp.sum(weight, axis=1, keepdims=True)
        weight = weight.astype(BF16)
        acc = jnp.zeros((32, HD), F32)
        for i in range(conts):
            part = jnp.dot(weight, cache[1, g * conts + i], preferred_element_type=F32)
            acc = jnp.where(owner_out == i, part, acc)
        both = jnp.where(lane[:, :HD] < 64, high, sums)
        for h in range(2):
            at = (g - start) // 2 * 64 + h * PER + half
            out[at : at + 16] = acc[h * 16 : h * 16 + 16]
            stats[at : at + 16] = both[h * 16 : h * 16 + 16]


def prefix_kernel(table, r0, r1, r2, r3, cache, out, held, scores, highs, totals, accs):
    lens = [table[20 + s] for s in range(4)]
    for e, ref in enumerate((r0, r1, r2, r3)):
        held[e] = ref[...]
    queries = [held[table[16 + s], s] for s in range(4)]

    def first(s, start, size, high):
        block = cache[0, s, pl.ds(start, size)]
        part = lax.dot_general(queries[s], block, CONTRACT, preferred_element_type=F32)
        lane = lax.broadcasted_iota(jnp.int32, (64, size), 1)
        part = jnp.where(lane < lens[s] - start, part, NEG)
        for c in range(size // HD):
            piece = part[:, c * HD : (c + 1) * HD]
            scores[s, start // HD + c] = piece
            high = piece if high is None else jnp.maximum(high, piece)
        return high

    def second(s, start, size, high, sums, acc):
        weights = []
        for c in range(size // HD):
            weight = jnp.exp2((scores[s, start // HD + c] - high) * (SCALE * LOG2E))
            sums = weight if sums is None else sums + weight
            weights.append(weight.astype(BF16))
        block = cache[1, s, pl.ds(start, size)]
        more = jnp.dot(jnp.concatenate(weights, axis=1), block, preferred_element_type=F32)
        return sums, more if acc is None else acc + more

    for s in range(4):
        highs[s] = first(s, 0, FIRST, None)
    for start, size in LATER:
        for s in range(4):

            @pl.when(lens[s] > start)
            def _():
                highs[s] = first(s, start, size, highs[s])

    for s in range(4):
        highs[s] = jnp.broadcast_to(jnp.max(highs[s], axis=1, keepdims=True), (64, HD))
    for s in range(4):
        totals[s], accs[s] = second(s, 0, FIRST, highs[s], None, None)
    for start, size in LATER:
        for s in range(4):

            @pl.when(lens[s] > start)
            def _():
                totals[s], accs[s] = second(s, start, size, highs[s], totals[s], accs[s])

    row = lax.broadcasted_iota(jnp.int32, (64, HD), 0)
    column_of = lax.broadcasted_iota(jnp.int32, (64, HD), 1)
    which = lax.broadcasted_iota(jnp.int32, (16, HD), 0)
    for s in range(4):
        sums = jnp.broadcast_to(jnp.sum(totals[s], axis=1, keepdims=True), (64, HD))
        out[s, :64] = (accs[s] / sums).astype(BF16)
        logs = highs[s] * SCALE + jnp.log(sums)
        line = jnp.sum(jnp.where(row == column_of, logs, 0.0), axis=0, keepdims=True)
        top = line.astype(BF16).astype(F32)
        middle = (line - top).astype(BF16).astype(F32)
        low = line - top - middle
        lines = jnp.where(
            which == 0, top, jnp.where(which == 1, middle, jnp.where(which == 2, low, 0.0))
        )
        out[s, 64:MSG] = lines.astype(BF16)


def prefix_scratch():
    part = pltpu.VMEM((4, 64, HD), F32)
    return [
        pltpu.VMEM((4, 4, 64, HD), BF16),
        pltpu.VMEM((4, PLEN // HD, 64, HD), F32),
        part,
        part,
        part,
    ]


def finish_kernel(
    ids, table, c0, c1, c2, c3, tail_out, tail_lse, w0, w1, w2, w3,
    scores, keep, send, held, attention, products,
):
    for e, ref in enumerate((c0, c1, c2, c3)):
        held[e] = ref[...]
    totals = [[], []]
    for j in range(4):
        message = held[table[40 + j], j]
        lines = message[64:MSG].astype(F32)
        line = (lines[0:1] + lines[1:2]) + lines[2:3]
        logs = column(line, 64)
        for h in range(2):
            rows = slice(j * PER, (j + 1) * PER)
            own = slice(j * 64 + h * PER, j * 64 + (h + 1) * PER)
            prefix_out = message[h * PER : (h + 1) * PER].astype(F32)
            prefix_lse = logs[h * PER : (h + 1) * PER]
            own_lse = tail_lse[own][:, 0:1]
            high = jnp.maximum(prefix_lse, own_lse)
            share_a = jnp.exp(prefix_lse - high)
            share_b = jnp.exp(own_lse - high)
            both = share_a + share_b
            merged = (share_a * prefix_out + share_b * tail_out[own]) / both
            attention[rows, h * HD : (h + 1) * HD] = merged.astype(BF16)
            totals[h].append(jnp.broadcast_to(high + jnp.log(both), (PER, HD)))
    diagonal = lax.broadcasted_iota(jnp.int32, (ROWS, HD), 0) == lax.broadcasted_iota(
        jnp.int32, (ROWS, HD), 1
    )
    for h in range(2):
        total = jnp.concatenate(totals[h], axis=0)
        scores[h : h + 1] = jnp.sum(jnp.where(diagonal, total, 0.0), axis=0, keepdims=True)
    a, b, core, x = ids[0], ids[1], ids[2], ids[3]
    left = attention[...]
    for ref, at_b in zip((w0, w1, w2, w3), around(b, True)):
        for d in (0, 2):
            right = jnp.concatenate(
                [
                    jnp.concatenate([ref[i, :, h * HD : (h + 1) * HD] for i in (d, d + 1)], axis=1)
                    for h in (2, 3)
                ],
                axis=0,
            )
            both = jnp.dot(left, right, preferred_element_type=F32)
            for i in range(2):
                at_a = lax.rem(a - d - i + 4, 4)
                block = jnp.where(core == 0, 4 * at_b + at_a, 4 * at_a + at_b)
                products[block] = both[:, i * HD : (i + 1) * HD]
    for pair in range(4):
        for side in range(2):
            keep[lax.rem(pair - x + 4, 4), side] = products[core * 8 + pair * 2 + side]
            send[pair, side] = products[(1 - core) * 8 + pair * 2 + side].astype(BF16)


def first_sum_kernel(ids, keep, got, o0, o1, o2, o3):
    x = ids[3]
    for d in range(4):
        total = keep[d] + got[lax.rem(x + d, 4)].astype(F32)
        if d == 0:
            o0[...] = total
        else:
            (o1, o2, o3)[d - 1][...] = total.astype(BF16)


def second_sum_kernel(ids, o0, g1, g2, g3, hidden, out):
    core, x = ids[2], ids[3]
    for side in range(2):
        total = o0[side] + (
            g1[side].astype(F32) + g2[side].astype(F32) + g3[side].astype(F32)
        )
        at = pl.multiple_of((core * 8 + x * 2 + side) * HD, HD)
        out[side] = (hidden[:, pl.ds(at, HD)].astype(F32) + total).astype(BF16)


def gather_kernel(ids, *refs):
    mine, other, out, sems = refs[:4], refs[4:8], refs[8], refs[9]
    core, x = ids[2], ids[3]
    copies = []
    for d in range(4):
        for side in range(2):
            at = lax.rem(x - d + 4, 4) * 2 + side
            for pieces, half in ((mine, core), (other, 1 - core)):
                columns = pl.ds(pl.multiple_of((half * 8 + at) * HD, HD), HD)
                copies.append(
                    pltpu.make_async_copy(
                        pieces[d].at[side], out.at[:, columns], sems.at[len(copies)]
                    )
                )
                copies[-1].start()
    for copy in copies:
        copy.wait()


def split(wide, core):
    z, y = wide // 4, wide % 4
    return jnp.where(core == 0, y, z), jnp.where(core == 0, z, y)


def gather_ring(value, first):
    return [value] + [shift(value, first, step) for step in (1, 2, 3)]


def choose(held, table, base, rows):
    shape = struct((4, rows, HD), BF16)
    sends = call(
        functools.partial(route_kernel, base),
        [shape] * 4,
        [table] + held,
        smem=(0,),
        scratch=[pltpu.VMEM((16, rows, HD), BF16)],
    )
    return [sends[0]] + [shift(sends[step], False, step) for step in (1, 2, 3)]


def body(
    hidden_in, attn_gain, w_qkv, q_gain, k_gain, w_out,
    prefix_cache, tail_cache, prompt_lens, tail_lens, slot_prompt,
):
    wide = lax.axis_index("wide").astype(jnp.int32)
    narrow = lax.axis_index("narrow").astype(jnp.int32)
    core, x = narrow % 2, narrow // 2
    a, b = split(wide, core)
    ids = jnp.stack([a, b, core, x]).astype(jnp.int32)

    channel = jnp.arange(HD, dtype=jnp.int32)
    inverse_freq = jnp.exp((channel % 64).astype(F32) * (-2.0 / HD) * math.log(1000000.0))
    table, angles = call(
        tables_kernel,
        [struct((64,), jnp.int32), struct((ROWS, HD), F32)],
        [ids, slot_prompt, prompt_lens, tail_lens, inverse_freq.reshape(1, HD)],
        smem=(0, 1, 2, 3),
        smem_out=(0,),
        scratch=[pltpu.SMEM((64,), jnp.int32)],
    )
    cosine = jnp.cos(angles)
    sine = jnp.sin(angles) * jnp.where(channel < HD // 2, -1.0, 1.0)[None, :]
    q_gain, k_gain = q_gain.reshape(1, HD), k_gain.reshape(1, HD)

    mixed = call(
        mix_kernel,
        struct((ROWS, 6 * HD), BF16),
        [w_qkv, w_out],
        hbm=(0, 1),
        scratch=[pltpu.SemaphoreType.DMA((3,))],
        grant=60 << 20,
    )
    near = gather_ring(mixed, True)
    normed = call(
        norm_kernel,
        struct((16, ROWS, HD), BF16),
        [hidden_in, attn_gain.reshape(1, -1)],
        cost=(HINT, 1 << 20),
    )
    near, normed, table = lax.optimization_barrier((near, normed, table))
    near_query, near_other = call(
        pack_kernel, [struct((4, ROWS, 2 * HD), BF16), struct((4, ROWS, 4 * HD), BF16)], near
    )
    far_query = gather_ring(near_query, False)
    beside = shift_pair(near_other, False)
    far_other = [near_other, beside, shift_pair(near_other, True), shift_pair(beside, True)]
    queries = call(
        query_kernel,
        struct((4, 64, HD), BF16),
        [ids, normed] + far_query + [q_gain, cosine, sine],
        smem=(0,),
        cost=(2 * ROWS * 256 * 2048, 2 << 20),
    )

    held = gather_ring(queries, True)
    tails = []
    for start in (0, 4):
        tails.append(
            call(
                functools.partial(tail_kernel, start),
                [struct((HD, HD), F32)] * 2,
                [tail_lens, queries, tail_cache],
                smem=(0,),
                cost=(2 * 64 * 32 * TLEN * HD, 4 << 20),
            )
        )
    held, tails[0] = lax.optimization_barrier((held, tails[0]))
    asked = choose(held, table, 0, 64)
    asked, tails[1] = lax.optimization_barrier((asked, tails[1]))
    results = call(
        prefix_kernel,
        struct((4, MSG, HD), BF16),
        [table] + asked + [prefix_cache],
        smem=(0,),
        scratch=prefix_scratch(),
        cost=(2 * 2 * 4 * 64 * PLEN * HD, 8 << 20),
    )
    held = gather_ring(results, True)
    new_cache, tail_out, tail_lse = call(
        own_kernel,
        [struct((2, ROWS, HD), BF16)] + [struct((2 * HD, HD), F32)] * 2,
        [ids, normed] + far_other + [k_gain, cosine, sine, queries, *tails[0], *tails[1]],
        smem=(0,),
        cost=(2 * ROWS * 256 * 2048, 3 << 20),
    )
    held, tail_out = lax.optimization_barrier((held, tail_out))
    homes = choose(held, table, 24, MSG)

    scores, keep, send = call(
        finish_kernel,
        [
            struct((2, ROWS), F32),
            struct((4, 2, ROWS, HD), F32),
            struct((4, 2, ROWS, HD), BF16),
        ],
        [ids, table] + homes + [tail_out, tail_lse] + far_other,
        smem=(0, 1),
        scratch=[pltpu.VMEM((4, 4, MSG, HD), BF16), pltpu.VMEM((ROWS, 2 * HD), BF16),
            pltpu.VMEM((16, ROWS, HD), F32),
        ],
        cost=(2 * ROWS * 256 * 2048, 3 << 20),
    )
    got = swap_core(send)
    block = struct((2, ROWS, HD), BF16)
    sums = call(
        first_sum_kernel,
        [struct((2, ROWS, HD), F32), block, block, block],
        [ids, keep, got],
        smem=(0,),
    )
    moved = [shift_x(sums[step], step) for step in (1, 2, 3)]
    mine = call(second_sum_kernel, block, [ids, sums[0]] + moved + [hidden_in], smem=(0,))
    ours = [mine] + [shift_x(mine, step) for step in (1, 2, 3)]
    theirs = [swap_core(piece) for piece in ours]
    hidden_out = call(gather_kernel, struct((ROWS, 2048), BF16), [ids] + ours + theirs, smem=(0,), hbm_out=True,
        scratch=[pltpu.SemaphoreType.DMA((16,))],
    )
    return (hidden_out, scores.T, new_cache)


def solution(mesh):
    in_specs = (
        P("wide", None),
        P(),
        P("wide", "narrow"),
        P(),
        P(),
        P("narrow", "wide"),
        P(None, "wide", None, "narrow"),
        P(None, "wide", None, "narrow"),
        P(),
        P("wide"),
        P(),
    )
    out_specs = (P("wide", None), P("wide", "narrow"), P(None, "wide", "narrow"))
    return jax.shard_map(body, mesh=mesh, in_specs=in_specs, out_specs=out_specs, check_vma=False)
```
